1024 devices in a mesh: sect: 4 (over x), grp: 64 (over z, core), span: 4 (over y).
Axes of the slice: x: 4, y: 4, z: 32, core: 2. Of those that a mesh axis runs over, the one named last changes fastest.
Arguments:
- grad_out: bfloat16 [5120, 8192], P('grp', 'span'), may hold values from -6 to 6
- destination: int32 [5120], P('grp'), may hold values from 0 to 5119, as said below
- w_down: bfloat16 [5120, 8192], P('sect', 'span'), may hold values from -0.078125 to 0.078125
- pre_act: bfloat16 [5120, 5120], P('grp', ('sect', 'span')), may hold values from -6 to 6
- w_up: bfloat16 [5120, 5120], P(None, ('sect', 'span')), may hold values from -0.078125 to 0.078125
- queries: bfloat16 [20480, 1280], P('grp', ('sect', 'span')), may hold values from -16 to 16
- key_states: bfloat16 [20480, 1280], P('grp', ('sect', 'span')), may hold values from -16 to 16
- value_states: bfloat16 [20480, 1280], P('grp', ('sect', 'span')), may hold values from -6 to 6
- lengths: int32 [192], replicated, may hold values from 1 to 80, 5120 in all
Outputs:
- grad_queries: bfloat16 [20480, 1280], P('grp', ('sect', 'span'))
- grad_keys: bfloat16 [20480, 1280], P('grp', ('sect', 'span'))
- grad_values: bfloat16 [20480, 1280], P('grp', ('sect', 'span'))
The draws below stay inside these ranges and needn't reach their ends.
Inputs may be any that keep to these rules, and one draw needn't show every extreme that they name: `destination`: a permutation of the merged tokens; the merged tokens on one index of grp go to exactly 40 indices of grp, exactly 2 to each. `lengths`: an image has 4 patches for each merged token; images lie one after another along the merged tokens.
All inputs are finite; a program needn't handle non-finite values.
Results may differ from the reference program's by a relative error of at most 0.015.
Values may be sent and summed in bfloat16 or wider, within the bound.
A program may use at most 64 MiB of HBM per device.

```python
import math
import jax
import jax.numpy as jnp
import numpy as np
from jax import lax

HEADS = 16
HEAD_DIM = 80
MERGED = 8192
MERGED_DEV = 80
WIDTH = 1280
MERGE_IN = 5120
TOKENS = 5120
PATCHES = 20480
IMAGES = 192
OFFS = 40
CAP = 2


def draw_destination(key, part):
    groups = TOKENS // MERGED_DEV
    ranks = jax.random.permutation(jax.random.fold_in(key, 1), groups).astype(jnp.int32)
    candidates = jnp.arange(groups, dtype=jnp.int32)
    priority = jnp.where(candidates == groups // 2, -2, jnp.where(candidates == 1 % groups, -1, ranks))
    shifts = jnp.argsort(priority, stable=True)[:OFFS].astype(jnp.int32)
    sources = jnp.arange(groups, dtype=jnp.int32)[:, None]
    slot_ids = jnp.arange(MERGED_DEV, dtype=jnp.int32)[None, :]
    classes = slot_ids // CAP
    targets = (sources + shifts[classes]) % groups
    positions = targets * MERGED_DEV + slot_ids
    orders = jax.vmap(lambda sub_key: jax.random.permutation(sub_key, MERGED_DEV))(jax.random.split(jax.random.fold_in(key, 2), groups))
    return jnp.take_along_axis(positions, orders, axis=1).reshape(-1).astype(jnp.int32)


def base_rows(key, salt_value):
    drawn = jnp.clip(jax.random.normal(jax.random.fold_in(key, salt_value), (PATCHES, HEADS * HEAD_DIM), jnp.float32), -4.0, 4.0)
    return drawn


def draw_queries(key, part):
    drawn = base_rows(key, 11)
    return drawn.astype(jnp.bfloat16)


def draw_key_states(key, part):
    drawn = base_rows(key, 21)
    return drawn.astype(jnp.bfloat16)


def block_scale(rng, dims, shards, smallest, top_value):
    loudness = 1.0
    for dim, blocks in shards:
        steps = jax.random.uniform(jax.random.fold_in(jax.random.fold_in(rng, 6), dim), (blocks,), jnp.float32, smallest / len(shards), top_value / len(shards))
        loudness = loudness * jnp.repeat(jnp.exp(steps), dims[dim] // blocks).reshape((-1,) + (1,) * (len(dims) - 1 - dim))
    return loudness


def length_profile(amount, total, most, slope):
    loads = [(1 << 20) // math.isqrt(grade ** slope) + 1 for grade in range(2, amount + 1)]
    rest, counts = total - most - (amount - 1), [1] * (amount - 1)
    while rest > 0:
        free = [i for i in range(amount - 1) if counts[i] < most]
        whole, budget = sum([loads[i] for i in free]), rest
        for i in free:
            more = min(most - counts[i], max(1, budget * loads[i] // whole), rest)
            counts[i] = counts[i] + more
            rest = rest - more
    return np.array([most] + counts)


def ragged(own_key, number_of, total, most, skew):
    if number_of == 2:
        one = jax.random.randint(own_key, (), max(1, total - most), min(most, total - 1) + 1)
        return jnp.stack([one, total - one])
    sizes = jnp.asarray(length_profile(number_of, total, most, skew), jnp.int32)
    pairs = (number_of - 1) // 2
    source_of, receiver = sizes[1:1 + 2 * pairs:2], sizes[2:2 + 2 * pairs:2]
    margin = jnp.minimum(source_of - 1, most - receiver)
    moved = jax.random.randint(jax.random.fold_in(own_key, 1), (pairs,), 0, 1 << 20) % (margin + 1)
    sizes = sizes.at[1:1 + 2 * pairs:2].set(source_of - moved).at[2:2 + 2 * pairs:2].set(receiver + moved)
    return sizes[jax.random.permutation(jax.random.fold_in(own_key, 2), number_of)]


def scatter_about(rng, shape, scale, limit, pieces=(), kind=jnp.bfloat16):
    entries = jax.random.normal(rng, shape, jnp.float32) * scale
    if len(pieces) > 0:
        entries = block_scale(rng, shape, pieces, -0.22, 0.18) * entries
    return jnp.clip(entries, min=-limit, max=limit).astype(kind)


def setup_inputs(seed: int = 0) -> dict:
    splits = jax.random.split(jax.random.key(seed), 10)
    return {
        "grad_out": scatter_about(splits[0], (TOKENS, MERGED), 1.0, 6.0, ((0, 64), (1, 4))),
        "destination": draw_destination(jax.random.fold_in(splits[9], 71), 0),
        "w_down": scatter_about(splits[2], (MERGE_IN, MERGED), MERGE_IN ** -0.5, 0.078125, ((0, 4), (1, 4))),
        "pre_act": scatter_about(splits[3], (TOKENS, MERGE_IN), 1.5, 6.0, ((0, 64), (1, 16))),
        "w_up": scatter_about(splits[4], (MERGE_IN, MERGE_IN), MERGE_IN ** -0.5, 0.078125, ((1, 16),)),
        "queries": draw_queries(jax.random.fold_in(splits[9], 71), 0),
        "key_states": draw_key_states(jax.random.fold_in(splits[9], 71), 0),
        "value_states": scatter_about(splits[7], (PATCHES, WIDTH), 1.0, 6.0, ((0, 64), (1, 16))),
        "lengths": ragged(splits[8], IMAGES, TOKENS, MERGED_DEV, 2).astype(jnp.int32),
    }


def gelu_slope(values):
    normal_cdf = 0.5 * (1.0 + jax.scipy.special.erf(values * 0.7071067811865476))
    return normal_cdf + values * jnp.exp(-0.5 * values * values) * 0.3989422804014327


def reference(grad_out, destination, w_down, pre_act, w_up, queries, key_states, value_states, lengths):
    grad_enc = jnp.zeros_like(grad_out).at[destination].set(grad_out)
    grad_hidden = lax.dot_general(grad_enc, w_down, (((1,), (1,)), ((), ())), preferred_element_type=jnp.float32)
    grad_pre = (grad_hidden * gelu_slope(pre_act.astype(jnp.float32))).astype(jnp.bfloat16)
    grad_merge = lax.dot_general(grad_pre, w_up, (((1,), (1,)), ((), ())), preferred_element_type=jnp.float32)
    grad_attn = grad_merge.reshape(PATCHES, WIDTH).astype(jnp.bfloat16)
    boundaries = jnp.cumsum(lengths).astype(jnp.int32)
    positions = jnp.arange(TOKENS, dtype=jnp.int32)
    token_image = jnp.sum((boundaries[None, :] <= positions[:, None]).astype(jnp.int32), 1)
    patch_image = jnp.repeat(token_image, 4)
    block = 4 * MERGED_DEV
    blocks = PATCHES // block
    keys_padded = jnp.pad(key_states, ((block, block), (0, 0)))
    values_padded = jnp.pad(value_states, ((block, block), (0, 0)))
    image_padded = jnp.pad(patch_image, (block, block), constant_values=-1)
    scale = HEAD_DIM ** -0.5

    def one_block(carry, index):
        key_total, value_total = carry
        start = (index * block).astype(jnp.int32)
        query_heads = lax.dynamic_slice_in_dim(queries, start, block, 0).reshape(block, HEADS, HEAD_DIM).astype(jnp.float32)
        grad_heads = lax.dynamic_slice_in_dim(grad_attn, start, block, 0).reshape(block, HEADS, HEAD_DIM).astype(jnp.float32)
        near_keys = lax.dynamic_slice_in_dim(keys_padded, start, 3 * block, 0).reshape(3 * block, HEADS, HEAD_DIM).astype(jnp.float32)
        near_values = lax.dynamic_slice_in_dim(values_padded, start, 3 * block, 0).reshape(3 * block, HEADS, HEAD_DIM).astype(jnp.float32)
        query_image = lax.dynamic_slice_in_dim(patch_image, start, block, 0)
        key_image = lax.dynamic_slice_in_dim(image_padded, start, 3 * block, 0)
        same_image = query_image[:, None] == key_image[None, :]
        scores = jnp.einsum('qhe,khe->hqk', query_heads, near_keys) * scale
        scores = jnp.where(same_image[None], scores, -jnp.inf)
        top_score = jnp.max(scores, -1, keepdims=True)
        weights = jnp.exp(scores - top_score)
        probs = weights / jnp.sum(weights, -1, keepdims=True)
        probs_low = probs.astype(jnp.bfloat16).astype(jnp.float32)
        attended = jnp.einsum('hqk,khe->qhe', probs_low, near_values)
        row_delta = jnp.sum(grad_heads * attended, -1)
        value_part = jnp.einsum('hqk,qhe->khe', probs_low, grad_heads)
        grad_probs = jnp.einsum('qhe,khe->hqk', grad_heads, near_values)
        grad_scores = (probs * (grad_probs - row_delta.T[:, :, None])).astype(jnp.bfloat16).astype(jnp.float32)
        grad_query = (jnp.einsum('hqk,khe->qhe', grad_scores, near_keys) * scale).astype(jnp.bfloat16)
        key_part = jnp.einsum('hqk,qhe->khe', grad_scores, query_heads) * scale
        key_total = lax.dynamic_update_slice_in_dim(key_total, lax.dynamic_slice_in_dim(key_total, start, 3 * block, 0) + key_part.reshape(3 * block, WIDTH), start, 0)
        value_total = lax.dynamic_update_slice_in_dim(value_total, lax.dynamic_slice_in_dim(value_total, start, 3 * block, 0) + value_part.reshape(3 * block, WIDTH), start, 0)
        return (key_total, value_total), grad_query.reshape(block, WIDTH)

    zeros_total = jnp.zeros((PATCHES + 2 * block, WIDTH), jnp.float32)
    (key_total, value_total), grad_blocks = lax.scan(one_block, (zeros_total, zeros_total), jnp.arange(blocks, dtype=jnp.int32))
    grad_queries = grad_blocks.reshape(PATCHES, WIDTH)
    grad_keys = key_total[block:block + PATCHES].astype(jnp.bfloat16)
    grad_values = value_total[block:block + PATCHES].astype(jnp.bfloat16)
    return (grad_queries, grad_keys, grad_values)
```

```python
import jax
import jax.numpy as jnp
from jax import lax
from jax.sharding import PartitionSpec as P

HEAD_DIM = 80


def passed_along(block, axis, distance):
    devices = range(lax.axis_size(axis))
    route = [(i - distance, i) for i in devices if i - distance in devices]
    return lax.ppermute(block, axis, route)


def extended(x, sides, width):
    for axis, dim in sides:
        peers, length = (lax.axis_size(axis), x.shape[dim])
        up = [(i, (i + 1) % peers) for i in range(peers - 1)]
        down = [(j, i) for i, j in up]
        last = lax.slice_in_dim(x, length - width, length, axis=dim)
        first = lax.slice_in_dim(x, 0, width, axis=dim)
        before = lax.ppermute(last, axis, up)
        after = lax.ppermute(first, axis, down)
        x = jnp.concatenate([before, x, after], axis=dim)
    return x


def gelu_slope(values):
    normal_cdf = 0.5 * (1.0 + jax.scipy.special.erf(values * 0.7071067811865476))
    return normal_cdf + values * jnp.exp(-0.5 * values * values) * 0.3989422804014327


def packing(destination, groups, row_count):
    offsets = min(groups, row_count // 2)
    capacity = row_count // offsets
    targets = destination // row_count
    slot_ids = destination % row_count
    order = jnp.arange(row_count, dtype=jnp.int32)
    earlier = (targets[:, None] == targets[None, :]) & (order[:, None] < order[None, :])
    index = targets * capacity + jnp.sum(earlier.astype(jnp.int32), 0)
    slots = jnp.arange(groups * capacity, dtype=jnp.int32)
    return (index[None, :] == slots[:, None]).astype(jnp.bfloat16), slot_ids


def send_back(terms, offset_by):
    return passed_along(terms.astype(jnp.bfloat16), "grp", offset_by).astype(terms.dtype)


def on_device(
    grad_out, destination, w_down, pre_act, w_up, queries, key_states, value_states, lengths
):
    groups = lax.axis_size("grp")
    merged_rows = grad_out.shape[0]
    contract_last = (((1,), (1,)), ((), ()))
    spans = lax.axis_size("span")
    sects = lax.axis_size("sect")
    local_hidden = w_up.shape[1]
    partial_hidden = lax.dot_general(
        grad_out, w_down, contract_last, preferred_element_type=jnp.float32
    ).astype(jnp.bfloat16)
    sent = partial_hidden.reshape(merged_rows, spans, local_hidden).transpose(1, 0, 2)
    terms = lax.all_to_all(sent, "span", split_axis=0, concat_axis=0, tiled=True)
    rows = jnp.sum(terms.astype(jnp.float32), 0).astype(jnp.bfloat16)
    packer, slot_ids = packing(destination, groups, merged_rows)
    labelled = jnp.concatenate(
        [rows, (slot_ids + 1).astype(jnp.bfloat16)[:, None], jnp.zeros((merged_rows, 63), jnp.bfloat16)], 1
    )
    packed = jnp.dot(packer, labelled, preferred_element_type=jnp.float32).astype(jnp.bfloat16)
    arrived = lax.all_to_all(packed, "grp", split_axis=0, concat_axis=0, tiled=True)
    label = arrived[:, local_hidden].astype(jnp.int32)
    unpacker = (
        label[None, :] == jnp.arange(1, merged_rows + 1, dtype=jnp.int32)[:, None]
    ).astype(jnp.bfloat16)
    grad_hidden = jnp.dot(
        unpacker, arrived[:, :local_hidden], preferred_element_type=jnp.float32
    )
    grad_pre = (grad_hidden * gelu_slope(pre_act.astype(jnp.float32))).astype(jnp.bfloat16)
    head_devices = sects * spans
    merge_rows = w_up.shape[0]
    head_cols = queries.shape[1]
    heads_here = head_cols // HEAD_DIM
    merged = lax.dot_general(
        w_up, grad_pre, contract_last, preferred_element_type=jnp.float32
    ).astype(jnp.bfloat16)
    merged = merged.reshape(4, sects, spans, head_cols, merged_rows).transpose(1, 2, 0, 3, 4)
    first = lax.all_to_all(merged, "sect", split_axis=0, concat_axis=0, tiled=True)
    first = jnp.sum(first.astype(jnp.float32), 0).astype(jnp.bfloat16)
    second = lax.all_to_all(first, "span", split_axis=0, concat_axis=0, tiled=True)
    share = jnp.sum(second.astype(jnp.float32), 0)
    patches = 4 * merged_rows
    grad_attn = (
        share.reshape(4, head_cols, merged_rows)
        .transpose(2, 0, 1)
        .reshape(patches, head_cols)
        .astype(jnp.bfloat16)
    )
    stacked = jnp.stack([key_states, value_states])
    widened = extended(stacked, (("grp", 1),), patches)
    near_keys = widened[0].reshape(3 * patches, heads_here, HEAD_DIM)
    near_values = widened[1].reshape(3 * patches, heads_here, HEAD_DIM)
    group_index = lax.axis_index("grp")
    positions = (group_index - 1) * merged_rows + jnp.arange(3 * merged_rows, dtype=jnp.int32)
    boundaries = jnp.cumsum(lengths)
    token_image = jnp.sum((boundaries[None, :] <= positions[:, None]).astype(jnp.int32), 1)
    inside = (positions >= 0) & (positions < merged_rows * groups)
    token_image = jnp.where(inside, token_image, -1)
    key_image = jnp.repeat(token_image, 4)
    query_image = key_image[patches : 2 * patches]
    same_image = query_image[:, None] == key_image[None, :]
    query_heads = queries.reshape(patches, heads_here, HEAD_DIM)
    grad_heads = grad_attn.reshape(patches, heads_here, HEAD_DIM)
    scale = HEAD_DIM ** (-0.5)
    scores = (
        jnp.einsum("qhe,khe->hqk", query_heads, near_keys, preferred_element_type=jnp.float32)
        * scale
    )
    scores = jnp.where(same_image[None], scores, -jnp.inf)
    top_score = jnp.max(scores, -1, keepdims=True)
    weights = jnp.exp(scores - top_score)
    probs = weights / jnp.sum(weights, -1, keepdims=True)
    probs_low = probs.astype(jnp.bfloat16)
    attended = jnp.einsum(
        "hqk,khe->qhe", probs_low, near_values, preferred_element_type=jnp.float32
    )
    row_delta = jnp.sum(grad_heads.astype(jnp.float32) * attended, -1)
    value_part = jnp.einsum(
        "hqk,qhe->khe", probs_low, grad_heads, preferred_element_type=jnp.float32
    )
    grad_probs = jnp.einsum(
        "qhe,khe->hqk", grad_heads, near_values, preferred_element_type=jnp.float32
    )
    grad_scores = (probs * (grad_probs - row_delta.T[:, :, None])).astype(jnp.bfloat16)
    grad_query = (
        jnp.einsum("hqk,khe->qhe", grad_scores, near_keys, preferred_element_type=jnp.float32)
        * scale
    ).astype(jnp.bfloat16)
    key_part = (
        jnp.einsum("hqk,qhe->khe", grad_scores, query_heads, preferred_element_type=jnp.float32)
        * scale
    )
    parts = jnp.stack([key_part, value_part]).reshape(2, 3 * patches, head_cols)
    own_part = parts[:, patches : 2 * patches]
    from_right = send_back(parts[:, :patches], -1)
    from_left = send_back(parts[:, 2 * patches :], 1)
    totals = own_part + from_right + from_left
    return (
        grad_query.reshape(patches, head_cols),
        totals[0].astype(jnp.bfloat16),
        totals[1].astype(jnp.bfloat16),
    )


def solution(mesh):
    placed = (
        P("grp", "span"),
        P("grp"),
        P("sect", "span"),
        P("grp", ("sect", "span")),
        P(None, ("sect", "span")),
        P("grp", ("sect", "span")),
        P("grp", ("sect", "span")),
        P("grp", ("sect", "span")),
        P(),
    )
    return jax.shard_map(
        on_device,
        mesh=mesh,
        in_specs=placed,
        out_specs=(
            P("grp", ("sect", "span")),
            P("grp", ("sect", "span")),
            P("grp", ("sect", "span")),
        ),
        check_vma=False,
    )
```

```python
import functools

import jax
import jax.numpy as jnp
from jax import lax
from jax.experimental import pallas as pl
from jax.experimental.pallas import tpu as pltpu
from jax.sharding import PartitionSpec as P

HEAD_DIM = 80
LABEL_LANES = 64
BF16 = jnp.bfloat16
F32 = jnp.float32
LAST = (((1,), (1,)), ((), ()))
FIRST = (((0,), (0,)), ((), ()))


def dot(a, b, dims=(((1,), (0,)), ((), ()))):
    return lax.dot_general(a, b, dims, preferred_element_type=F32)


def iota(shape, dim):
    return lax.broadcasted_iota(jnp.int32, shape, dim)


def gelu_slope(values):
    normal_cdf = 0.5 * (1.0 + lax.erf(values * 0.7071067811865476))
    return normal_cdf + values * jnp.exp(-0.5 * values * values) * 0.3989422804014327


def far_first(n):
    return sorted(range(1, n), key=lambda d: -min(d, n - d))


def token_packing(dest, rows, near, far, cap):
    where_to = dest.astype(F32)
    group = jnp.floor((where_to + 0.5) * (1.0 / rows))
    place = where_to - group * rows
    square = (rows, rows)
    across = jnp.broadcast_to(group, square)
    down = jnp.sum(jnp.where(iota(square, 0) == iota(square, 1), across, 0.0), 1, keepdims=True)
    earlier = (down == across) & (iota(square, 0) < iota(square, 1))
    copy = jnp.sum(jnp.where(earlier, 1.0, 0.0), 0, keepdims=True)
    group_hi = jnp.floor((group + 0.5) * (1.0 / near))
    slot = (group - group_hi * near) * (far * cap) + group_hi * cap + copy
    slots = near * far * cap
    hit = iota((slots, rows), 0).astype(F32) == slot
    label = jnp.sum(jnp.where(hit, place + 1.0, 0.0), 1, keepdims=True)
    return jnp.where(hit, 1.0, 0.0).astype(BF16), label


def image_ids(lengths, group, rows, tokens):
    images = lengths.shape[1]
    square = (images, images)
    sizes = jnp.broadcast_to(lengths.astype(F32), square)
    row, col = iota(square, 0), iota(square, 1)
    sizes_down = jnp.sum(jnp.where(row == col, sizes, 0.0), 1, keepdims=True)
    ends_down = jnp.sum(jnp.where(col <= row, sizes, 0.0), 1, keepdims=True)
    ends_across = jnp.sum(jnp.where(row <= col, sizes_down, 0.0), 0, keepdims=True)
    base = group * rows
    own = (base + (iota((4 * rows, 1), 0) >> 2)).astype(F32)
    near = (base - rows + (iota((1, 12 * rows), 1) >> 2)).astype(F32)
    own_image = jnp.sum(jnp.where(ends_across <= own, 1.0, 0.0), 1, keepdims=True)
    near_image = jnp.sum(jnp.where(ends_down <= near, 1.0, 0.0), 0, keepdims=True)
    inside = (near >= 0.0) & (near < float(tokens))
    return own_image, jnp.where(inside, near_image, -1.0)


def kernel(
    sizes,
    grad_out,
    dest,
    w_down,
    pre_act,
    w_up,
    queries,
    keys,
    values,
    lengths,
    out_q,
    out_k,
    out_v,
    go,
    wd,
    wu,
    pre,
    qs,
    kx,
    vx,
    dst,
    lens,
    part,
    part_in,
    near_out,
    near_in,
    far_out,
    far_in,
    mix,
    mix_a,
    mix_b,
    fin_a,
    fin_b,
    sum_a,
    sum_b,
    back,
    back_in,
    probs,
    load_sem,
    down_sem,
    part_s,
    part_r,
    halo_s,
    halo_r,
    near_s,
    near_r,
    far_s,
    far_r,
    a1_s,
    a1_r,
    b1_s,
    b1_r,
    a2_s,
    a2_r,
    b2_s,
    b2_r,
    back_s,
    back_r,
):
    sects, groups, spans, near, far, cap, split = sizes
    rows = grad_out.shape[0]
    hidden = w_up.shape[1]
    cols = queries.shape[1]
    patches = 4 * rows
    x, g, y = lax.axis_index("sect"), lax.axis_index("grp"), lax.axis_index("span")
    g_hi, g_lo = g // near, g % near

    def at_x(d):
        return ((x + d) % sects, g, y)

    def at_y(d):
        return (x, g, (y + d) % spans)

    def at_near(d):
        return (x, g_hi * near + (g_lo + d) % near, y)

    def at_far(d):
        return (x, ((g_hi + d) % far) * near + g_lo, y)

    def at_g(d):
        return (x, (g + d + groups) % groups, y)

    barrier = pltpu.get_barrier_semaphore()
    peers = [at_far(d) for d in far_first(far)]
    peers += [at_y(d) for d in range(1, spans)]
    peers += [at_near(d) for d in range(1, near)]
    peers += [at_g(1), at_g(-1)]
    peers += [at_x(d) for d in range(1, sects)]
    for peer in peers:
        pl.semaphore_signal(barrier, inc=1, device_id=peer, device_id_type=pl.DeviceIdType.MESH)

    sent = []

    def send(src, to, send_sem, recv_sem, peer):
        copy = pltpu.make_async_remote_copy(
            src_ref=src,
            dst_ref=to,
            send_sem=send_sem,
            recv_sem=recv_sem,
            device_id=peer,
            device_id_type=pl.DeviceIdType.MESH,
        )
        copy.start()
        sent.append(copy)
        return copy

    def load(src, to, sem):
        copy = pltpu.make_async_copy(src, to, sem)
        copy.start()
        return copy

    order_y = far_first(spans) + [0]
    load_go = load(grad_out, go, load_sem.at[0])
    load_dst = load(dest, dst, load_sem.at[1])
    load_wd = []
    for d in order_y:
        chunk = pl.ds(pl.multiple_of(((y + d) % spans) * hidden, 16), hidden)
        load_wd.append(load(w_down.at[chunk, :], wd.at[chunk, :], down_sem.at[d]))
    load_len = load(lengths, lens, load_sem.at[2])
    load_q = load(queries, qs, load_sem.at[3])
    load_k = load(keys, kx.at[pl.ds(patches, patches), :], load_sem.at[4])
    load_v = load(values, vx.at[pl.ds(patches, patches), :], load_sem.at[5])
    load_pre = load(pre_act, pre, load_sem.at[6])
    head_devices = sects * spans
    for d in range(head_devices):
        for p in range(4):
            load(
                w_up.at[pl.ds((p * head_devices + d) * cols, cols), :],
                wu.at[pl.ds((d * 4 + p) * cols, cols), :],
                load_sem.at[7],
            )

    load_dst.wait()
    packer, label = token_packing(dst[...], rows, near, far, cap)
    load_go.wait()
    own_part = None
    for d, loaded in zip(order_y, load_wd):
        loaded.wait()
        chunk = pl.ds(pl.multiple_of(((y + d) % spans) * hidden, 16), hidden)
        product = dot(go[...], wd[chunk, :], LAST)
        if d == 0:
            own_part = product
        else:
            part[d - 1] = product.astype(BF16)
    load_len.wait()
    own_image, near_image = image_ids(lens[...], g, rows, rows * groups)
    load_k.wait()
    load_v.wait()

    pl.semaphore_wait(barrier, len(peers))
    part_copies = [
        send(part.at[d - 1], part_in.at[d - 1], part_s.at[d - 1], part_r.at[d - 1], at_y(d))
        for d in far_first(spans)
    ]
    own_block = pl.ds(patches, patches)
    halo_copies = []
    for i, (full, step) in enumerate(((kx, 1), (vx, 1), (kx, -1), (vx, -1))):
        land = pl.ds(0 if step == 1 else 2 * patches, patches)
        halo_copies.append(
            send(full.at[own_block, :], full.at[land, :], halo_s.at[i], halo_r.at[i], at_g(step))
        )

    total = own_part
    for d, copy in zip(far_first(spans), part_copies):
        copy.wait_recv()
        total = total + part_in[d - 1].astype(F32)
    slots = near * far * cap
    near_rows, far_rows = far * cap, near * cap
    near_out[:, :hidden] = dot(packer, total.astype(BF16)).astype(BF16)
    near_out[:, hidden:] = jnp.broadcast_to(label, (slots, LABEL_LANES)).astype(BF16)
    near_copies = []
    for d in range(near - 1, 0, -1):
        block = pl.ds(pl.multiple_of(((g_lo + d) % near) * near_rows, near_rows), near_rows)
        near_copies.append(
            send(
                near_out.at[block, :],
                near_in.at[pl.ds(d * near_rows, near_rows), :],
                near_s.at[d - 1],
                near_r.at[d - 1],
                at_near(d),
            )
        )
    mine = pl.ds(pl.multiple_of(g_lo * near_rows, near_rows), near_rows)
    near_in[pl.ds(0, near_rows), :] = near_out[mine, :]
    out_row = iota((slots, slots), 0)
    in_row = iota((slots, slots), 1)
    source = ((out_row // cap) % near) * near_rows + (out_row // far_rows) * cap + out_row % cap
    shuffle = jnp.where(source == in_row, 1.0, 0.0).astype(BF16)
    for copy in near_copies:
        copy.wait_recv()
    far_out[...] = dot(shuffle, near_in[...]).astype(BF16)
    far_copies = []
    for d in far_first(far):
        block = pl.ds(pl.multiple_of(((g_hi + d) % far) * far_rows, far_rows), far_rows)
        far_copies.append(
            send(
                far_out.at[block, :],
                far_in.at[pl.ds(d * far_rows, far_rows), :],
                far_s.at[d - 1],
                far_r.at[d - 1],
                at_far(d),
            )
        )
    mine = pl.ds(pl.multiple_of(g_hi * far_rows, far_rows), far_rows)
    far_in[pl.ds(0, far_rows), :] = far_out[mine, :]

    scale = HEAD_DIM ** (-0.5)
    load_q.wait()
    for copy in halo_copies:
        copy.wait_recv()
    scores = dot(qs[...], kx[...], LAST) * scale
    scores = jnp.where(own_image == near_image, scores, -jnp.inf)
    top_score = jnp.max(scores, 1, keepdims=True)
    weights = jnp.exp(scores - top_score)
    probs[...] = weights / jnp.sum(weights, 1, keepdims=True)
    attended = dot(probs[...].astype(BF16), vx[...])
    load_pre.wait()
    slope = gelu_slope(pre[...].astype(F32))
    pltpu.make_async_copy(w_up, wu, load_sem.at[7]).wait()

    for copy in far_copies:
        copy.wait_recv()
    arrived = far_in[...]
    place = arrived[:, hidden : hidden + 1].astype(F32)
    unpacker = jnp.where(place == (iota((slots, rows), 1) + 1).astype(F32), 1.0, 0.0)
    grad_hidden = dot(unpacker.astype(BF16), arrived[:, :hidden], FIRST)
    grad_pre = (grad_hidden * slope).astype(BF16)
    top, low = pl.ds(0, split), pl.ds(split, rows - split)
    width = 4 * cols
    a_copies, b_copies = {}, {}
    for dx in far_first(sects) + [0]:
        for dy in far_first(spans) + [0]:
            owner = ((x + dx) % sects) * spans + (y + dy) % spans
            weight = wu[pl.ds(pl.multiple_of(owner * width, 16), width), :]
            mix[dx, dy] = dot(grad_pre, weight, LAST).astype(BF16)
            if dx:
                a_copies[dx, dy] = send(
                    mix.at[dx, dy, top, :],
                    mix_a.at[dx - 1, dy],
                    a1_s.at[dx - 1, dy],
                    a1_r.at[dx - 1, dy],
                    at_x(dx),
                )
            if dy:
                b_copies[dx, dy] = send(
                    mix.at[dx, dy, low, :],
                    mix_b.at[dy - 1, dx],
                    b1_s.at[dy - 1, dx],
                    b1_r.at[dy - 1, dx],
                    at_y(dy),
                )
    a2_copies, b2_copies = [], []
    share_a = share_b = None
    for dy in far_first(spans) + [0]:
        total = mix[0, dy, top, :].astype(F32)
        for dx in far_first(sects):
            a_copies[dx, dy].wait_recv()
            total = total + mix_a[dx - 1, dy].astype(F32)
        if dy:
            sum_a[dy - 1] = total.astype(BF16)
            a2_copies.append(
                send(sum_a.at[dy - 1], fin_a.at[dy - 1], a2_s.at[dy - 1], a2_r.at[dy - 1], at_y(dy))
            )
        else:
            share_a = total
    for dx in far_first(sects) + [0]:
        total = mix[dx, 0, low, :].astype(F32)
        for dy in far_first(spans):
            b_copies[dx, dy].wait_recv()
            total = total + mix_b[dy - 1, dx].astype(F32)
        if dx:
            sum_b[dx - 1] = total.astype(BF16)
            b2_copies.append(
                send(sum_b.at[dx - 1], fin_b.at[dx - 1], b2_s.at[dx - 1], b2_r.at[dx - 1], at_x(dx))
            )
        else:
            share_b = total
    for copy in a2_copies + b2_copies:
        copy.wait_recv()
    for d in range(spans - 1):
        share_a = share_a + fin_a[d].astype(F32)
    for d in range(sects - 1):
        share_b = share_b + fin_b[d].astype(F32)
    share = jnp.concatenate([share_a, share_b], 0).astype(BF16)

    patch_row, token = iota((patches, rows), 0), iota((patches, rows), 1)
    grad_attn = jnp.zeros((patches, cols), F32)
    for p in range(4):
        spread = jnp.where(patch_row == 4 * token + p, 1.0, 0.0).astype(BF16)
        grad_attn = grad_attn + dot(spread, share[:, p * cols : (p + 1) * cols])
    row_delta = jnp.sum(grad_attn.astype(BF16).astype(F32) * attended, 1, keepdims=True)
    grad_attn = grad_attn.astype(BF16)
    grad_scores = []
    back_copies = []
    q = qs[...]
    kept = None
    for block in (0, 2, 1):
        lanes = pl.ds(block * patches, patches)
        weights = probs[:, lanes]
        grad_probs = dot(grad_attn, vx[lanes, :], LAST)
        score_part = (weights * (grad_probs - row_delta)).astype(BF16)
        value_part = dot(weights.astype(BF16), grad_attn, FIRST)
        key_part = dot(score_part, q, FIRST) * scale
        grad_scores.append((lanes, score_part))
        if block == 1:
            kept = key_part, value_part
        else:
            side = block // 2
            back[side, 0] = key_part.astype(BF16)
            back[side, 1] = value_part.astype(BF16)
            back_copies.append(
                send(
                    back.at[side],
                    back_in.at[1 - side],
                    back_s.at[side],
                    back_r.at[1 - side],
                    at_g(block - 1),
                )
            )
    grad_query = jnp.zeros((patches, cols), F32)
    for lanes, score_part in grad_scores:
        grad_query = grad_query + dot(score_part, kx[lanes, :])
    out_q[...] = (grad_query * scale).astype(BF16)
    key_part, value_part = kept
    for copy in back_copies:
        copy.wait_recv()
    for side in range(2):
        key_part = key_part + back_in[side, 0].astype(F32)
        value_part = value_part + back_in[side, 1].astype(F32)
    out_k[...] = key_part.astype(BF16)
    out_v[...] = value_part.astype(BF16)
    for copy in sent:
        copy.wait_send()


def on_device(
    grad_out, destination, w_down, pre_act, w_up, queries, key_states, value_states, lengths
):
    sects, groups, spans = (lax.axis_size(a) for a in ("sect", "grp", "span"))
    rows, merged = grad_out.shape
    merge_rows, hidden = w_up.shape
    cols = queries.shape[1]
    patches = 4 * rows
    near = 8 if groups % 8 == 0 and groups > 8 else 2
    far = groups // near
    cap = rows // min(groups, rows // 2)
    slots = groups * cap
    split = (rows * 5 // 8 // 16) * 16 if rows >= 32 else rows // 2
    width = 4 * cols
    wide = hidden + LABEL_LANES
    dma = pltpu.SemaphoreType.DMA
    vmem = pltpu.VMEM
    some = pl.BlockSpec(memory_space=pl.ANY)
    out = jax.ShapeDtypeStruct((patches, cols), BF16)
    sizes = (sects, groups, spans, near, far, cap, split)
    return pl.pallas_call(
        functools.partial(kernel, sizes),
        out_shape=(out, out, out),
        in_specs=[some] * 9,
        out_specs=[pl.BlockSpec(memory_space=pltpu.VMEM)] * 3,
        scratch_shapes=[
            vmem((rows, merged), BF16),
            vmem(w_down.shape, BF16),
            vmem((merge_rows, hidden), BF16),
            vmem((rows, hidden), BF16),
            vmem((patches, cols), BF16),
            vmem((3 * patches, cols), BF16),
            vmem((3 * patches, cols), BF16),
            vmem((1, rows), jnp.int32),
            vmem((1, lengths.shape[0]), jnp.int32),
            vmem((spans - 1, rows, hidden), BF16),
            vmem((spans - 1, rows, hidden), BF16),
            vmem((slots, wide), BF16),
            vmem((slots, wide), BF16),
            vmem((slots, wide), BF16),
            vmem((slots, wide), BF16),
            vmem((sects, spans, rows, width), BF16),
            vmem((sects - 1, spans, split, width), BF16),
            vmem((spans - 1, sects, rows - split, width), BF16),
            vmem((spans - 1, split, width), BF16),
            vmem((sects - 1, rows - split, width), BF16),
            vmem((spans - 1, split, width), BF16),
            vmem((sects - 1, rows - split, width), BF16),
            vmem((2, 2, patches, cols), BF16),
            vmem((2, 2, patches, cols), BF16),
            vmem((patches, 3 * patches), F32),
            dma((8,)),
            dma((spans,)),
            dma((spans - 1,)),
            dma((spans - 1,)),
            dma((4,)),
            dma((4,)),
            dma((near - 1,)),
            dma((near - 1,)),
            dma((far - 1,)),
            dma((far - 1,)),
            dma((sects - 1, spans)),
            dma((sects - 1, spans)),
            dma((spans - 1, sects)),
            dma((spans - 1, sects)),
            dma((spans - 1,)),
            dma((spans - 1,)),
            dma((sects - 1,)),
            dma((sects - 1,)),
            dma((2,)),
            dma((2,)),
        ],
        compiler_params=pltpu.CompilerParams(
            collective_id=0, has_side_effects=True, vmem_limit_bytes=60 * 1024 * 1024
        ),
        name="merger_attention_backward",
    )(
        grad_out,
        destination.reshape(1, rows),
        w_down,
        pre_act,
        w_up,
        queries,
        key_states,
        value_states,
        lengths.reshape(1, lengths.shape[0]),
    )


def solution(mesh):
    placed = (
        P("grp", "span"),
        P("grp"),
        P("sect", "span"),
        P("grp", ("sect", "span")),
        P(None, ("sect", "span")),
        P("grp", ("sect", "span")),
        P("grp", ("sect", "span")),
        P("grp", ("sect", "span")),
        P(),
    )
    return jax.shard_map(
        on_device,
        mesh=mesh,
        in_specs=placed,
        out_specs=(
            P("grp", ("sect", "span")),
            P("grp", ("sect", "span")),
            P("grp", ("sect", "span")),
        ),
        check_vma=False,
    )
```

```python
import functools

import jax
import jax.numpy as jnp
from jax import lax
from jax.experimental import pallas as pl
from jax.experimental.pallas import tpu as pltpu
from jax.sharding import PartitionSpec as P

HEAD_DIM = 80
LABEL_LANES = 64
BF16 = jnp.bfloat16
F32 = jnp.float32
LAST = (((1,), (1,)), ((), ()))
FIRST = (((0,), (0,)), ((), ()))


def dot(a, b, dims=(((1,), (0,)), ((), ()))):
    return lax.dot_general(a, b, dims, preferred_element_type=F32)


def iota(shape, dim):
    return lax.broadcasted_iota(jnp.int32, shape, dim)


def gelu_slope(values):
    normal_cdf = 0.5 * (1.0 + lax.erf(values * 0.7071067811865476))
    return normal_cdf + values * jnp.exp(-0.5 * values * values) * 0.3989422804014327


def far_first(n):
    return sorted(range(1, n), key=lambda d: -min(d, n - d))


def token_packing(dest, rows, near, far, cap):
    where_to = dest.astype(F32)
    group = jnp.floor((where_to + 0.5) * (1.0 / rows))
    place = where_to - group * rows
    square = (rows, rows)
    across = jnp.broadcast_to(group, square)
    down = jnp.sum(jnp.where(iota(square, 0) == iota(square, 1), across, 0.0), 1, keepdims=True)
    earlier = (down == across) & (iota(square, 0) < iota(square, 1))
    copy = jnp.sum(jnp.where(earlier, 1.0, 0.0), 0, keepdims=True)
    group_hi = jnp.floor((group + 0.5) * (1.0 / near))
    slot = (group - group_hi * near) * (far * cap) + group_hi * cap + copy
    slots = near * far * cap
    hit = iota((slots, rows), 0).astype(F32) == slot
    label = jnp.sum(jnp.where(hit, place + 1.0, 0.0), 1, keepdims=True)
    return jnp.where(hit, 1.0, 0.0).astype(BF16), label


def image_ids(lengths, group, rows, tokens):
    images = lengths.shape[1]
    square = (images, images)
    sizes = jnp.broadcast_to(lengths.astype(F32), square)
    row, col = iota(square, 0), iota(square, 1)
    sizes_down = jnp.sum(jnp.where(row == col, sizes, 0.0), 1, keepdims=True)
    ends_down = jnp.sum(jnp.where(col <= row, sizes, 0.0), 1, keepdims=True)
    ends_across = jnp.sum(jnp.where(row <= col, sizes_down, 0.0), 0, keepdims=True)
    base = group * rows
    own = (base + (iota((1, 4 * rows), 1) >> 2)).astype(F32)
    near = (base - rows + (iota((12 * rows, 1), 0) >> 2)).astype(F32)
    own_image = jnp.sum(jnp.where(ends_down <= own, 1.0, 0.0), 0, keepdims=True)
    near_image = jnp.sum(jnp.where(ends_across <= near, 1.0, 0.0), 1, keepdims=True)
    inside = (near >= 0.0) & (near < float(tokens))
    return own_image, jnp.where(inside, near_image, -1.0)


def kernel(
    sizes,
    grad_out,
    dest,
    w_down,
    pre_act,
    w_up,
    queries,
    keys,
    values,
    lengths,
    out_q,
    out_k,
    out_v,
    go,
    wd,
    wt,
    wu,
    pre,
    qs,
    kx,
    vx,
    dst,
    lens,
    part,
    part_in,
    near_out,
    near_in,
    far_out,
    far_in,
    mix,
    mix_a,
    mix_b,
    fin_a,
    fin_b,
    sum_a,
    sum_b,
    back,
    back_in,
    probs,
    probs_low,
    ready,
    load_sem,
    down_sem,
    part_s,
    part_r,
    halo_s,
    halo_r,
    near_s,
    near_r,
    far_s,
    far_r,
    a1_s,
    a1_r,
    b1_s,
    b1_r,
    a2_s,
    a2_r,
    b2_s,
    b2_r,
    back_s,
    back_r,
):
    sects, groups, spans, near, far, cap, split = sizes
    rows = grad_out.shape[0]
    hidden = w_up.shape[0]
    cols = queries.shape[0]
    patches = 4 * rows
    x, g, y = lax.axis_index("sect"), lax.axis_index("grp"), lax.axis_index("span")
    g_hi, g_lo = g // near, g % near

    def at_x(d):
        return ((x + d) % sects, g, y)

    def at_y(d):
        return (x, g, (y + d) % spans)

    def at_near(d):
        return (x, g_hi * near + (g_lo + d) % near, y)

    def at_far(d):
        return (x, ((g_hi + d) % far) * near + g_lo, y)

    def at_g(d):
        return (x, (g + d + groups) % groups, y)

    barrier = pltpu.get_barrier_semaphore()
    far_steps = sorted({1 % far, far - 1})
    peers = [at_far(d) for d in far_steps]
    peers += [at_y(d) for d in range(1, spans)]
    peers += [at_near(d) for d in range(1, near)]
    peers += [at_g(1), at_g(-1)]
    peers += [at_x(d) for d in range(1, sects)]
    def signal(sem, peer):
        pl.semaphore_signal(sem, inc=1, device_id=peer, device_id_type=pl.DeviceIdType.MESH)

    for peer in peers:
        signal(barrier, peer)

    sent = []

    def send(src, to, send_sem, recv_sem, peer):
        copy = pltpu.make_async_remote_copy(
            src_ref=src,
            dst_ref=to,
            send_sem=send_sem,
            recv_sem=recv_sem,
            device_id=peer,
            device_id_type=pl.DeviceIdType.MESH,
        )
        copy.start()
        sent.append(copy)
        return copy

    def load(src, to, sem):
        copy = pltpu.make_async_copy(src, to, sem)
        copy.start()
        return copy

    order_y = far_first(spans) + [0]
    load_go = load(grad_out, go, load_sem.at[0])
    load_dst = load(dest, dst, load_sem.at[1])
    load_wd = []
    for d in order_y:
        chunk = pl.ds(pl.multiple_of(((y + d) % spans) * hidden, 16), hidden)
        load_wd.append(load(w_down.at[chunk, :], wd.at[chunk, :], down_sem.at[d]))
    load_len = load(lengths, lens, load_sem.at[2])
    load_q = load(queries, qs, load_sem.at[3])
    load_k = load(keys, kx.at[1], load_sem.at[4])
    load_v = load(values, vx.at[1], load_sem.at[5])
    load_pre = load(pre_act, pre, load_sem.at[6])
    load_wt = load(w_up, wt, load_sem.at[7])

    load_dst.wait()
    packer, label = token_packing(dst[...], rows, near, far, cap)
    load_k.wait()
    load_v.wait()
    pl.semaphore_wait(barrier, len(peers))
    for i, d in enumerate(far_steps):
        signal(ready.at[0, i], at_far(d))
    halo_copies = []
    for i, (full, step) in enumerate(((kx, 1), (vx, 1), (kx, -1), (vx, -1))):
        land = full.at[0 if step == 1 else 2]
        halo_copies.append(send(full.at[1], land, halo_s.at[i], halo_r.at[i], at_g(step)))

    load_go.wait()
    own_part = None
    part_copies = []
    for d, loaded in zip(order_y, load_wd):
        loaded.wait()
        chunk = pl.ds(pl.multiple_of(((y + d) % spans) * hidden, 16), hidden)
        product = dot(go[...], wd[chunk, :], LAST)
        if d == 0:
            own_part = product
        else:
            part[d - 1] = product.astype(BF16)
            part_copies.append(
                send(part.at[d - 1], part_in.at[d - 1], part_s.at[d - 1], part_r.at[d - 1], at_y(d))
            )
    load_len.wait()
    own_image, near_image = image_ids(lens[...], g, rows, rows * groups)
    for i in range(len(far_steps)):
        pl.semaphore_wait(ready.at[0, i], 1)
    second = [d for d in (1, far - 1, 2, far - 2) if far > 2 and d < far]
    second = sorted(set(second))
    for i, d in enumerate(second):
        signal(ready.at[1, i], at_far(d))

    total = own_part
    for d, copy in zip(far_first(spans), part_copies):
        copy.wait_recv()
        total = total + part_in[d - 1].astype(F32)
    slots = near * far * cap
    near_rows, far_rows = far * cap, near * cap
    near_out[:, :hidden] = dot(packer, total.astype(BF16)).astype(BF16)
    near_out[:, hidden:] = jnp.broadcast_to(label, (slots, LABEL_LANES)).astype(BF16)
    near_copies = []
    for d in range(near - 1, 0, -1):
        block = pl.ds(pl.multiple_of(((g_lo + d) % near) * near_rows, near_rows), near_rows)
        near_copies.append(
            send(
                near_out.at[block, :],
                near_in.at[pl.ds(d * near_rows, near_rows), :],
                near_s.at[d - 1],
                near_r.at[d - 1],
                at_near(d),
            )
        )
    mine = pl.ds(pl.multiple_of(g_lo * near_rows, near_rows), near_rows)
    near_in[pl.ds(0, near_rows), :] = near_out[mine, :]
    out_row = iota((slots, slots), 0)
    in_row = iota((slots, slots), 1)
    source = ((out_row // cap) % near) * near_rows + (out_row // far_rows) * cap + out_row % cap
    shuffle = jnp.where(source == in_row, 1.0, 0.0).astype(BF16)
    for copy in near_copies:
        copy.wait_recv()
    far_out[...] = dot(shuffle, near_in[...]).astype(BF16)
    for i in range(len(second)):
        pl.semaphore_wait(ready.at[1, i], 1)
    far_copies = []
    for d in far_first(far):
        block = pl.ds(pl.multiple_of(((g_hi + d) % far) * far_rows, far_rows), far_rows)
        far_copies.append(
            send(
                far_out.at[block, :],
                far_in.at[pl.ds(d * far_rows, far_rows), :],
                far_s.at[d - 1],
                far_r.at[d - 1],
                at_far(d),
            )
        )
    mine = pl.ds(pl.multiple_of(g_hi * far_rows, far_rows), far_rows)
    far_in[pl.ds(0, far_rows), :] = far_out[mine, :]

    scale = HEAD_DIM ** (-0.5)
    width = 4 * cols
    load_q.wait()
    for copy in halo_copies:
        copy.wait_recv()
    top_score = None
    for block in range(3):
        scores = dot(kx[block], qs[...], FIRST) * scale
        image = near_image[block * patches : (block + 1) * patches]
        scores = jnp.where(image == own_image, scores, -jnp.inf)
        probs[block] = scores
        top = jnp.max(scores, 0, keepdims=True)
        top_score = top if top_score is None else jnp.maximum(top_score, top)
    weight_sum = jnp.zeros((1, patches), F32)
    for block in range(3):
        weights = jnp.exp(probs[block] - top_score)
        probs[block] = weights
        weight_sum = weight_sum + jnp.sum(weights, 0, keepdims=True)
    attended = jnp.zeros((cols, patches), F32)
    for block in range(3):
        weights = probs[block] / weight_sum
        probs[block] = weights
        probs_low[block] = weights.astype(BF16)
        attended = attended + dot(vx[block], probs_low[block])
    load_pre.wait()
    slope = gelu_slope(pre[...].astype(F32))
    load_wt.wait()
    step_rows = 32

    def regroup(i, carry):
        some = pl.ds(pl.multiple_of(i * step_rows, step_rows), step_rows)
        for d in range(sects * spans):
            for p in range(4):
                start = (p * sects * spans + d) * cols
                wu[d, some, p * cols : (p + 1) * cols] = wt[some, start : start + cols]
        return carry

    lax.fori_loop(0, hidden // step_rows, regroup, 0)

    for copy in far_copies:
        copy.wait_recv()
    arrived = far_in[...]
    place = arrived[:, hidden : hidden + 1].astype(F32)
    unpacker = jnp.where(place == (iota((slots, rows), 1) + 1).astype(F32), 1.0, 0.0)
    grad_hidden = dot(unpacker.astype(BF16), arrived[:, :hidden], FIRST)
    grad_pre = (grad_hidden * slope).astype(BF16)
    top, low = pl.ds(0, split), pl.ds(split, rows - split)
    a_copies, b_copies = {}, {}
    for dx in far_first(sects) + [0]:
        for dy in far_first(spans) + [0]:
            owner = ((x + dx) % sects) * spans + (y + dy) % spans
            mix[dx, dy] = dot(grad_pre, wu[owner]).astype(BF16)
            if dx:
                a_copies[dx, dy] = send(
                    mix.at[dx, dy, top, :],
                    mix_a.at[dx - 1, dy],
                    a1_s.at[dx - 1, dy],
                    a1_r.at[dx - 1, dy],
                    at_x(dx),
                )
            if dy:
                b_copies[dx, dy] = send(
                    mix.at[dx, dy, low, :],
                    mix_b.at[dy - 1, dx],
                    b1_s.at[dy - 1, dx],
                    b1_r.at[dy - 1, dx],
                    at_y(dy),
                )
    a2_copies, b2_copies = [], []
    share_a = share_b = None
    for dy in far_first(spans) + [0]:
        total = mix[0, dy, top, :].astype(F32)
        for dx in far_first(sects):
            a_copies[dx, dy].wait_recv()
            total = total + mix_a[dx - 1, dy].astype(F32)
        if dy:
            sum_a[dy - 1] = total.astype(BF16)
            a2_copies.append(
                send(sum_a.at[dy - 1], fin_a.at[dy - 1], a2_s.at[dy - 1], a2_r.at[dy - 1], at_y(dy))
            )
        else:
            share_a = total
    for dx in far_first(sects) + [0]:
        total = mix[dx, 0, low, :].astype(F32)
        for dy in far_first(spans):
            b_copies[dx, dy].wait_recv()
            total = total + mix_b[dy - 1, dx].astype(F32)
        if dx:
            sum_b[dx - 1] = total.astype(BF16)
            b2_copies.append(
                send(sum_b.at[dx - 1], fin_b.at[dx - 1], b2_s.at[dx - 1], b2_r.at[dx - 1], at_x(dx))
            )
        else:
            share_b = total
    for copy in a2_copies + b2_copies:
        copy.wait_recv()
    for d in range(spans - 1):
        share_a = share_a + fin_a[d].astype(F32)
    for d in range(sects - 1):
        share_b = share_b + fin_b[d].astype(F32)
    share = jnp.concatenate([share_a, share_b], 0).astype(BF16)

    token, patch = iota((rows, patches), 0), iota((rows, patches), 1)
    grad_attn = jnp.zeros((cols, patches), F32)
    for p in range(4):
        spread = jnp.where(patch == 4 * token + p, 1.0, 0.0).astype(BF16)
        grad_attn = grad_attn + dot(share[:, p * cols : (p + 1) * cols], spread, FIRST)
    row_delta = jnp.sum(grad_attn * attended, 0, keepdims=True)
    grad_attn = grad_attn.astype(BF16)
    back_copies = []
    q = qs[...]
    kept = None
    grad_query = jnp.zeros((cols, patches), F32)
    for block in (0, 2, 1):
        grad_probs = dot(vx[block], grad_attn, FIRST)
        score_part = (probs[block] * (grad_probs - row_delta)).astype(BF16)
        value_part = dot(grad_attn, probs_low[block], LAST)
        key_part = dot(q, score_part, LAST) * scale
        if block == 1:
            kept = key_part, value_part
        else:
            side = block // 2
            back[side, 0] = key_part.astype(BF16)
            back[side, 1] = value_part.astype(BF16)
            back_copies.append(
                send(
                    back.at[side],
                    back_in.at[1 - side],
                    back_s.at[side],
                    back_r.at[1 - side],
                    at_g(block - 1),
                )
            )
        grad_query = grad_query + dot(kx[block], score_part)
    out_q[...] = (grad_query * scale).astype(BF16)
    key_part, value_part = kept
    for copy in back_copies:
        copy.wait_recv()
    for side in range(2):
        key_part = key_part + back_in[side, 0].astype(F32)
        value_part = value_part + back_in[side, 1].astype(F32)
    out_k[...] = key_part.astype(BF16)
    out_v[...] = value_part.astype(BF16)
    for copy in sent:
        copy.wait_send()


def on_device(
    grad_out, destination, w_down, pre_act, w_up, queries, key_states, value_states, lengths
):
    sects, groups, spans = (lax.axis_size(a) for a in ("sect", "grp", "span"))
    rows, merged = grad_out.shape
    merge_rows, hidden = w_up.shape
    cols = queries.shape[1]
    patches = 4 * rows
    near = 8 if groups % 8 == 0 and groups > 8 else 2
    far = groups // near
    cap = rows // min(groups, rows // 2)
    slots = groups * cap
    split = (rows * 5 // 8 // 16) * 16 if rows >= 32 else rows // 2
    width = 4 * cols
    wide = hidden + LABEL_LANES
    dma = pltpu.SemaphoreType.DMA
    vmem = pltpu.VMEM
    some = pl.BlockSpec(memory_space=pl.ANY)
    out = jax.ShapeDtypeStruct((cols, patches), BF16)
    sizes = (sects, groups, spans, near, far, cap, split)
    outs = pl.pallas_call(
        functools.partial(kernel, sizes),
        out_shape=(out, out, out),
        in_specs=[some] * 9,
        out_specs=[pl.BlockSpec(memory_space=pltpu.VMEM)] * 3,
        scratch_shapes=[
            vmem((rows, merged), BF16),
            vmem(w_down.shape, BF16),
            vmem((hidden, merge_rows), BF16),
            vmem((sects * spans, hidden, width), BF16),
            vmem((rows, hidden), BF16),
            vmem((cols, patches), BF16),
            vmem((3, cols, patches), BF16),
            vmem((3, cols, patches), BF16),
            vmem((1, rows), jnp.int32),
            vmem((1, lengths.shape[0]), jnp.int32),
            vmem((spans - 1, rows, hidden), BF16),
            vmem((spans - 1, rows, hidden), BF16),
            vmem((slots, wide), BF16),
            vmem((slots, wide), BF16),
            vmem((slots, wide), BF16),
            vmem((slots, wide), BF16),
            vmem((sects, spans, rows, width), BF16),
            vmem((sects - 1, spans, split, width), BF16),
            vmem((spans - 1, sects, rows - split, width), BF16),
            vmem((spans - 1, split, width), BF16),
            vmem((sects - 1, rows - split, width), BF16),
            vmem((spans - 1, split, width), BF16),
            vmem((sects - 1, rows - split, width), BF16),
            vmem((2, 2, cols, patches), BF16),
            vmem((2, 2, cols, patches), BF16),
            vmem((3, patches, patches), F32),
            vmem((3, patches, patches), BF16),
            pltpu.SemaphoreType.REGULAR((2, 4)),
            dma((8,)),
            dma((spans,)),
            dma((spans - 1,)),
            dma((spans - 1,)),
            dma((4,)),
            dma((4,)),
            dma((near - 1,)),
            dma((near - 1,)),
            dma((far - 1,)),
            dma((far - 1,)),
            dma((sects - 1, spans)),
            dma((sects - 1, spans)),
            dma((spans - 1, sects)),
            dma((spans - 1, sects)),
            dma((spans - 1,)),
            dma((spans - 1,)),
            dma((sects - 1,)),
            dma((sects - 1,)),
            dma((2,)),
            dma((2,)),
        ],
        compiler_params=pltpu.CompilerParams(
            collective_id=0, has_side_effects=True, vmem_limit_bytes=60 * 1024 * 1024
        ),
        name="merger_attention_backward",
    )(
        grad_out,
        destination.reshape(1, rows),
        w_down,
        pre_act,
        w_up.T,
        queries.T,
        key_states.T,
        value_states.T,
        lengths.reshape(1, lengths.shape[0]),
    )
    return tuple(each.T for each in outs)


def solution(mesh):
    placed = (
        P("grp", "span"),
        P("grp"),
        P("sect", "span"),
        P("grp", ("sect", "span")),
        P(None, ("sect", "span")),
        P("grp", ("sect", "span")),
        P("grp", ("sect", "span")),
        P("grp", ("sect", "span")),
        P(),
    )
    return jax.shard_map(
        on_device,
        mesh=mesh,
        in_specs=placed,
        out_specs=(
            P("grp", ("sect", "span")),
            P("grp", ("sect", "span")),
            P("grp", ("sect", "span")),
        ),
        check_vma=False,
    )
```

```python
import functools

import jax
import jax.numpy as jnp
from jax import lax
from jax.experimental import pallas as pl
from jax.experimental.pallas import tpu as pltpu
from jax.sharding import PartitionSpec as P

HEAD_DIM = 80
LABEL_LANES = 64
BF16 = jnp.bfloat16
F32 = jnp.float32
LAST = (((1,), (1,)), ((), ()))
FIRST = (((0,), (0,)), ((), ()))


def dot(a, b, dims=(((1,), (0,)), ((), ()))):
    return lax.dot_general(a, b, dims, preferred_element_type=F32)


def iota(shape, dim):
    return lax.broadcasted_iota(jnp.int32, shape, dim)


def gelu_slope(values):
    normal_cdf = 0.5 * (1.0 + lax.erf(values * 0.7071067811865476))
    return normal_cdf + values * jnp.exp(-0.5 * values * values) * 0.3989422804014327


def log2(n):
    return n.bit_length() - 1


def far_first(n):
    return sorted(range(1, n), key=lambda d: -min(d, n - d))


def token_packing(dest, rows, near, far, cap):
    where_to = dest.astype(F32)
    group = jnp.floor((where_to + 0.5) * (1.0 / rows))
    place = where_to - group * rows
    square = (rows, rows)
    across = jnp.broadcast_to(group, square)
    down = jnp.sum(jnp.where(iota(square, 0) == iota(square, 1), across, 0.0), 1, keepdims=True)
    earlier = (down == across) & (iota(square, 0) < iota(square, 1))
    copy = jnp.sum(jnp.where(earlier, 1.0, 0.0), 0, keepdims=True)
    group_hi = jnp.floor((group + 0.5) * (1.0 / near))
    slot = (group - group_hi * near) * (far * cap) + group_hi * cap + copy
    slots = near * far * cap
    hit = iota((slots, rows), 0).astype(F32) == slot
    label = jnp.sum(jnp.where(hit, place + 1.0, 0.0), 1, keepdims=True)
    return jnp.where(hit, 1.0, 0.0).astype(BF16), label


def image_ids(lengths, group, rows, tokens):
    images = lengths.shape[1]
    square = (images, images)
    sizes = jnp.broadcast_to(lengths.astype(F32), square)
    row, col = iota(square, 0), iota(square, 1)
    sizes_down = jnp.sum(jnp.where(row == col, sizes, 0.0), 1, keepdims=True)
    ends_down = jnp.sum(jnp.where(col <= row, sizes, 0.0), 1, keepdims=True)
    ends_across = jnp.sum(jnp.where(row <= col, sizes_down, 0.0), 0, keepdims=True)
    base = group * rows
    own = (base + (iota((1, 4 * rows), 1) >> 2)).astype(F32)
    near = (base - rows + (iota((12 * rows, 1), 0) >> 2)).astype(F32)
    own_image = jnp.sum(jnp.where(ends_down <= own, 1.0, 0.0), 0, keepdims=True)
    near_image = jnp.sum(jnp.where(ends_across <= near, 1.0, 0.0), 1, keepdims=True)
    inside = (near >= 0.0) & (near < float(tokens))
    return own_image, jnp.where(inside, near_image, -1.0)


def kernel(
    sizes,
    grad_out,
    dest,
    w_down,
    pre_act,
    w_up,
    queries,
    keys,
    values,
    lengths,
    out_q,
    out_k,
    out_v,
    go,
    wd,
    wt,
    wu,
    pre,
    qs,
    kx,
    vx,
    dst,
    lens,
    part,
    part_in,
    near_out,
    near_in,
    far_out,
    far_in,
    mix,
    mix_a,
    mix_b,
    fin_a,
    fin_b,
    sum_a,
    sum_b,
    back,
    back_in,
    probs,
    probs_low,
    pack,
    swap,
    spread,
    slopes,
    own_part,
    ready,
    load_sem,
    down_sem,
    part_s,
    part_r,
    halo_s,
    halo_r,
    near_s,
    near_r,
    far_s,
    far_r,
    a1_s,
    a1_r,
    b1_s,
    b1_r,
    a2_s,
    a2_r,
    b2_s,
    b2_r,
    back_s,
    back_r,
):
    sects, groups, spans, near, far, cap, split = sizes
    rows = grad_out.shape[0]
    hidden = w_up.shape[0]
    cols = queries.shape[0]
    patches = 4 * rows
    x, g, y = lax.axis_index("sect"), lax.axis_index("grp"), lax.axis_index("span")
    g_hi, g_lo = g // near, g % near

    def at_x(d):
        return ((x + d) % sects, g, y)

    def at_y(d):
        return (x, g, (y + d) % spans)

    def at_near(d):
        return (x, g_hi * near + (g_lo + d) % near, y)

    def at_far(d):
        return (x, ((g_hi + d) % far) * near + g_lo, y)

    def at_g(d):
        return (x, (g + d + groups) % groups, y)

    sent = []

    def send(src, to, send_sem, recv_sem, peer):
        copy = pltpu.make_async_remote_copy(
            src_ref=src,
            dst_ref=to,
            send_sem=send_sem,
            recv_sem=recv_sem,
            device_id=peer,
            device_id_type=pl.DeviceIdType.MESH,
        )
        copy.start()
        sent.append(copy)
        return copy

    def load(src, to, sem):
        copy = pltpu.make_async_copy(src, to, sem)
        copy.start()
        return copy

    order_y = far_first(spans) + [0]
    load_go = load(grad_out, go, load_sem.at[0])
    load_dst = load(dest, dst, load_sem.at[1])
    load_wd = []
    load_k = load(keys, kx.at[1], load_sem.at[4])
    load_v = load(values, vx.at[1], load_sem.at[5])
    for d in order_y:
        chunk = pl.ds(pl.multiple_of(((y + d) % spans) * hidden, 16), hidden)
        load_wd.append(load(w_down.at[chunk, :], wd.at[chunk, :], down_sem.at[d]))
    load_len = load(lengths, lens, load_sem.at[2])
    load_q = load(queries, qs, load_sem.at[3])
    load_pre = load(pre_act, pre, load_sem.at[6])
    load_wt = load(w_up, wt, load_sem.at[7])

    barrier = pltpu.get_barrier_semaphore()
    far_steps = sorted({1 % far, far - 1})
    peers = [at_far(d) for d in far_steps]
    peers += [at_y(d) for d in range(1, spans)]
    peers += [at_near(d) for d in range(1, near)]
    peers += [at_g(1), at_g(-1)]
    peers += [at_x(d) for d in range(1, sects)]
    def signal(sem, peer):
        pl.semaphore_signal(sem, inc=1, device_id=peer, device_id_type=pl.DeviceIdType.MESH)

    for peer in peers:
        signal(barrier, peer)

    load_go.wait()
    part_copies = []
    for d, loaded in zip(order_y, load_wd):
        loaded.wait()
        chunk = pl.ds(pl.multiple_of(((y + d) % spans) * hidden, 16), hidden)
        product = dot(go[...], wd[chunk, :], LAST)
        if d == 0:
            own_part[...] = product
            continue
        part[d - 1] = product.astype(BF16)
        if not part_copies:
            pl.semaphore_wait(barrier, len(peers))
            for i, step in enumerate(far_steps):
                signal(ready.at[0, i], at_far(step))
        part_copies.append(
            send(part.at[d - 1], part_in.at[d - 1], part_s.at[d - 1], part_r.at[d - 1], at_y(d))
        )
    load_k.wait()
    load_v.wait()
    halo_copies = []
    for i, (full, step) in enumerate(((kx, 1), (vx, 1), (kx, -1), (vx, -1))):
        land = full.at[0 if step == 1 else 2]
        halo_copies.append(send(full.at[1], land, halo_s.at[i], halo_r.at[i], at_g(step)))
    load_dst.wait()
    pack[...], label = token_packing(dst[...], rows, near, far, cap)
    near_out[:, hidden:] = jnp.broadcast_to(label, (near * far * cap, LABEL_LANES)).astype(BF16)
    slots = near * far * cap
    near_rows, far_rows = far * cap, near * cap
    out_row = iota((slots, slots), 0)
    in_row = iota((slots, slots), 1)
    source = ((out_row >> log2(cap)) & (near - 1)) * near_rows
    source = source + (out_row >> log2(far_rows)) * cap + (out_row & (cap - 1))
    swap[...] = jnp.where(source == in_row, 1.0, 0.0).astype(BF16)
    for i in range(len(far_steps)):
        pl.semaphore_wait(ready.at[0, i], 1)
    second = [d for d in (1, far - 1, 2, far - 2) if far > 2 and d < far]
    second = sorted(set(second))
    for i, d in enumerate(second):
        signal(ready.at[1, i], at_far(d))

    total = own_part[...]
    for d, copy in zip(far_first(spans), part_copies):
        copy.wait_recv()
        total = total + part_in[d - 1].astype(F32)
    near_out[:, :hidden] = dot(pack[...], total.astype(BF16)).astype(BF16)
    near_copies = []
    for d in range(near - 1, 0, -1):
        block = pl.ds(pl.multiple_of(((g_lo + d) % near) * near_rows, near_rows), near_rows)
        near_copies.append(
            send(
                near_out.at[block, :],
                near_in.at[pl.ds(d * near_rows, near_rows), :],
                near_s.at[d - 1],
                near_r.at[d - 1],
                at_near(d),
            )
        )
    mine = pl.ds(pl.multiple_of(g_lo * near_rows, near_rows), near_rows)
    near_in[pl.ds(0, near_rows), :] = near_out[mine, :]
    for copy in near_copies:
        copy.wait_recv()
    far_out[...] = dot(swap[...], near_in[...]).astype(BF16)
    for i in range(len(second)):
        pl.semaphore_wait(ready.at[1, i], 1)
    far_copies = []

    def release(d):
        block = pl.ds(pl.multiple_of(((g_hi + d) % far) * far_rows, far_rows), far_rows)
        far_copies.append(
            send(
                far_out.at[block, :],
                far_in.at[pl.ds(d * far_rows, far_rows), :],
                far_s.at[d - 1],
                far_r.at[d - 1],
                at_far(d),
            )
        )
    waves = [[d for d in far_first(far) if min(d, far - d) == k] for k in range(far // 2, 0, -1)]
    waves += [[]] * (4 - len(waves))
    for d in waves[0] + waves[1]:
        release(d)
    mine = pl.ds(pl.multiple_of(g_hi * far_rows, far_rows), far_rows)
    far_in[pl.ds(0, far_rows), :] = far_out[mine, :]

    scale = HEAD_DIM ** (-0.5)
    width = 4 * cols
    load_q.wait()
    for copy in halo_copies:
        copy.wait_recv()
    load_len.wait()
    own_image, near_image = image_ids(lens[...], g, rows, rows * groups)
    top_score = None
    for block in range(3):
        scores = dot(kx[block], qs[...], FIRST) * scale
        image = near_image[block * patches : (block + 1) * patches]
        scores = jnp.where(image == own_image, scores, -jnp.inf)
        probs[block] = scores
        top = jnp.max(scores, 0, keepdims=True)
        top_score = top if top_score is None else jnp.maximum(top_score, top)
    weight_sum = jnp.zeros((1, patches), F32)
    for block in range(3):
        weights = jnp.exp(probs[block] - top_score)
        probs[block] = weights
        weight_sum = weight_sum + jnp.sum(weights, 0, keepdims=True)
    attended = jnp.zeros((cols, patches), F32)
    for block in range(3):
        weights = probs[block] / weight_sum
        probs[block] = weights
        probs_low[block] = weights.astype(BF16)
        attended = attended + dot(vx[block], probs_low[block])
    for d in waves[2]:
        release(d)
    load_pre.wait()
    slopes[...] = gelu_slope(pre[...].astype(F32))
    token, patch = iota((rows, patches), 0), iota((rows, patches), 1)
    for p in range(4):
        spread[p] = jnp.where(patch == 4 * token + p, 1.0, 0.0).astype(BF16)
    load_wt.wait()
    step_rows = 32

    def regroup(i, carry):
        some = pl.ds(pl.multiple_of(i * step_rows, step_rows), step_rows)
        for d in range(sects * spans):
            for p in range(4):
                start = (p * sects * spans + d) * cols
                wu[d, some, p * cols : (p + 1) * cols] = wt[some, start : start + cols]
        return carry

    lax.fori_loop(0, hidden // step_rows, regroup, 0)

    for d in waves[3]:
        release(d)

    for copy in far_copies:
        copy.wait_recv()
    arrived = far_in[...]
    place = arrived[:, hidden : hidden + 1].astype(F32)
    unpacker = jnp.where(place == (iota((slots, rows), 1) + 1).astype(F32), 1.0, 0.0)
    grad_hidden = dot(unpacker.astype(BF16), arrived[:, :hidden], FIRST)
    grad_pre = (grad_hidden * slopes[...]).astype(BF16)
    top, low = pl.ds(0, split), pl.ds(split, rows - split)
    a_copies, b_copies = {}, {}
    for dx in far_first(sects) + [0]:
        for dy in far_first(spans) + [0]:
            owner = ((x + dx) % sects) * spans + (y + dy) % spans
            mix[dx, dy] = dot(grad_pre, wu[owner]).astype(BF16)
            if dx:
                a_copies[dx, dy] = send(
                    mix.at[dx, dy, top, :],
                    mix_a.at[dx - 1, dy],
                    a1_s.at[dx - 1, dy],
                    a1_r.at[dx - 1, dy],
                    at_x(dx),
                )
            if dy:
                b_copies[dx, dy] = send(
                    mix.at[dx, dy, low, :],
                    mix_b.at[dy - 1, dx],
                    b1_s.at[dy - 1, dx],
                    b1_r.at[dy - 1, dx],
                    at_y(dy),
                )
    a2_copies, b2_copies = [], []

    def sum_top(dy):
        total = mix[0, dy, top, :].astype(F32)
        for dx in far_first(sects):
            a_copies[dx, dy].wait_recv()
            total = total + mix_a[dx - 1, dy].astype(F32)
        return total

    def sum_low(dx):
        total = mix[dx, 0, low, :].astype(F32)
        for dy in far_first(spans):
            b_copies[dx, dy].wait_recv()
            total = total + mix_b[dy - 1, dx].astype(F32)
        return total

    for d in far_first(sects):
        sum_b[d - 1] = sum_low(d).astype(BF16)
        b2_copies.append(
            send(sum_b.at[d - 1], fin_b.at[d - 1], b2_s.at[d - 1], b2_r.at[d - 1], at_x(d))
        )
    for d in far_first(spans):
        sum_a[d - 1] = sum_top(d).astype(BF16)
        a2_copies.append(
            send(sum_a.at[d - 1], fin_a.at[d - 1], a2_s.at[d - 1], a2_r.at[d - 1], at_y(d))
        )
    share_b, share_a = sum_low(0), sum_top(0)
    for copy in a2_copies + b2_copies:
        copy.wait_recv()
    for d in range(spans - 1):
        share_a = share_a + fin_a[d].astype(F32)
    for d in range(sects - 1):
        share_b = share_b + fin_b[d].astype(F32)
    share = jnp.concatenate([share_a, share_b], 0).astype(BF16)

    grad_attn = jnp.zeros((cols, patches), F32)
    for p in range(4):
        grad_attn = grad_attn + dot(share[:, p * cols : (p + 1) * cols], spread[p], FIRST)
    row_delta = jnp.sum(grad_attn * attended, 0, keepdims=True)
    grad_attn = grad_attn.astype(BF16)
    back_copies = []
    q = qs[...]
    kept = None
    grad_query = jnp.zeros((cols, patches), F32)
    for block in (0, 2, 1):
        grad_probs = dot(vx[block], grad_attn, FIRST)
        score_part = (probs[block] * (grad_probs - row_delta)).astype(BF16)
        value_part = dot(grad_attn, probs_low[block], LAST)
        key_part = dot(q, score_part, LAST) * scale
        if block == 1:
            kept = key_part, value_part
        else:
            side = block // 2
            back[side, 0] = key_part.astype(BF16)
            back[side, 1] = value_part.astype(BF16)
            back_copies.append(
                send(
                    back.at[side],
                    back_in.at[1 - side],
                    back_s.at[side],
                    back_r.at[1 - side],
                    at_g(block - 1),
                )
            )
        grad_query = grad_query + dot(kx[block], score_part)
    out_q[...] = (grad_query * scale).astype(BF16)
    key_part, value_part = kept
    for copy in back_copies:
        copy.wait_recv()
    for side in range(2):
        key_part = key_part + back_in[side, 0].astype(F32)
        value_part = value_part + back_in[side, 1].astype(F32)
    out_k[...] = key_part.astype(BF16)
    out_v[...] = value_part.astype(BF16)
    for copy in sent:
        copy.wait_send()


def move(*refs):
    half = len(refs) // 2
    for source, target in zip(refs[:half], refs[half:]):
        target[...] = source[...]


def on_device(
    grad_out, destination, w_down, pre_act, w_up, queries, key_states, value_states, lengths
):
    sects, groups, spans = (lax.axis_size(a) for a in ("sect", "grp", "span"))
    rows, merged = grad_out.shape
    merge_rows, hidden = w_up.shape
    cols = queries.shape[1]
    patches = 4 * rows
    near = 8 if groups % 8 == 0 and groups > 8 else 2
    far = groups // near
    cap = rows // min(groups, rows // 2)
    slots = groups * cap
    split = (rows * 5 // 8 // 16) * 16 if rows >= 32 else rows // 2
    width = 4 * cols
    wide = hidden + LABEL_LANES
    dma = pltpu.SemaphoreType.DMA
    vmem = pltpu.VMEM
    some = pl.BlockSpec(memory_space=pl.ANY)
    out = jax.ShapeDtypeStruct((cols, patches), BF16)
    sizes = (sects, groups, spans, near, far, cap, split)
    outs = pl.pallas_call(
        functools.partial(kernel, sizes),
        out_shape=(out, out, out),
        in_specs=[some] * 9,
        out_specs=[pl.BlockSpec(memory_space=pltpu.VMEM)] * 3,
        scratch_shapes=[
            vmem((rows, merged), BF16),
            vmem(w_down.shape, BF16),
            vmem((hidden, merge_rows), BF16),
            vmem((sects * spans, hidden, width), BF16),
            vmem((rows, hidden), BF16),
            vmem((cols, patches), BF16),
            vmem((3, cols, patches), BF16),
            vmem((3, cols, patches), BF16),
            vmem((1, rows), jnp.int32),
            vmem((1, lengths.shape[0]), jnp.int32),
            vmem((spans - 1, rows, hidden), BF16),
            vmem((spans - 1, rows, hidden), BF16),
            vmem((slots, wide), BF16),
            vmem((slots, wide), BF16),
            vmem((slots, wide), BF16),
            vmem((slots, wide), BF16),
            vmem((sects, spans, rows, width), BF16),
            vmem((sects - 1, spans, split, width), BF16),
            vmem((spans - 1, sects, rows - split, width), BF16),
            vmem((spans - 1, split, width), BF16),
            vmem((sects - 1, rows - split, width), BF16),
            vmem((spans - 1, split, width), BF16),
            vmem((sects - 1, rows - split, width), BF16),
            vmem((2, 2, cols, patches), BF16),
            vmem((2, 2, cols, patches), BF16),
            vmem((3, patches, patches), F32),
            vmem((3, patches, patches), BF16),
            vmem((slots, rows), BF16),
            vmem((slots, slots), BF16),
            vmem((4, rows, patches), BF16),
            vmem((rows, hidden), F32),
            vmem((rows, hidden), F32),
            pltpu.SemaphoreType.REGULAR((2, 4)),
            dma((8,)),
            dma((spans,)),
            dma((spans - 1,)),
            dma((spans - 1,)),
            dma((4,)),
            dma((4,)),
            dma((near - 1,)),
            dma((near - 1,)),
            dma((far - 1,)),
            dma((far - 1,)),
            dma((sects - 1, spans)),
            dma((sects - 1, spans)),
            dma((spans - 1, sects)),
            dma((spans - 1, sects)),
            dma((spans - 1,)),
            dma((spans - 1,)),
            dma((sects - 1,)),
            dma((sects - 1,)),
            dma((2,)),
            dma((2,)),
        ],
        compiler_params=pltpu.CompilerParams(
            collective_id=0, has_side_effects=True, vmem_limit_bytes=60 * 1024 * 1024
        ),
        name="merger_attention_backward",
    )(
        grad_out,
        destination.reshape(1, rows),
        w_down,
        pre_act,
        w_up.T,
        queries.T,
        key_states.T,
        value_states.T,
        lengths.reshape(1, lengths.shape[0]),
    )
    outs = pl.pallas_call(
        move,
        out_shape=(out, out, out),
        in_specs=[pl.BlockSpec(memory_space=pltpu.VMEM)] * 3,
        out_specs=[pl.BlockSpec(memory_space=pltpu.VMEM)] * 3,
        name="gradients_out",
    )(*outs)
    return tuple(each.T for each in outs)


def solution(mesh):
    placed = (
        P("grp", "span"),
        P("grp"),
        P("sect", "span"),
        P("grp", ("sect", "span")),
        P(None, ("sect", "span")),
        P("grp", ("sect", "span")),
        P("grp", ("sect", "span")),
        P("grp", ("sect", "span")),
        P(),
    )
    return jax.shard_map(
        on_device,
        mesh=mesh,
        in_specs=placed,
        out_specs=(
            P("grp", ("sect", "span")),
            P("grp", ("sect", "span")),
            P("grp", ("sect", "span")),
        ),
        check_vma=False,
    )
```

```python
import functools

import jax
import jax.numpy as jnp
from jax import lax
from jax.experimental import pallas as pl
from jax.experimental.pallas import tpu as pltpu
from jax.sharding import PartitionSpec as P

HEAD_DIM = 80
LABEL_LANES = 64
BF16 = jnp.bfloat16
F32 = jnp.float32
LAST = (((1,), (1,)), ((), ()))
FIRST = (((0,), (0,)), ((), ()))


def dot(a, b, dims=(((1,), (0,)), ((), ()))):
    return lax.dot_general(a, b, dims, preferred_element_type=F32)


def iota(shape, dim):
    return lax.broadcasted_iota(jnp.int32, shape, dim)


def gelu_slope(values):
    normal_cdf = 0.5 * (1.0 + lax.erf(values * 0.7071067811865476))
    return normal_cdf + values * jnp.exp(-0.5 * values * values) * 0.3989422804014327


def log2(n):
    return n.bit_length() - 1


def far_first(n):
    return sorted(range(1, n), key=lambda d: -min(d, n - d))


def token_packing(dest, rows, near, far, cap):
    where_to = dest.astype(F32)
    group = jnp.floor((where_to + 0.5) * (1.0 / rows))
    place = where_to - group * rows
    square = (rows, rows)
    across = jnp.broadcast_to(group, square)
    down = jnp.sum(jnp.where(iota(square, 0) == iota(square, 1), across, 0.0), 1, keepdims=True)
    earlier = (down == across) & (iota(square, 0) < iota(square, 1))
    copy = jnp.sum(jnp.where(earlier, 1.0, 0.0), 0, keepdims=True)
    group_hi = jnp.floor((group + 0.5) * (1.0 / near))
    slot = (group - group_hi * near) * (far * cap) + group_hi * cap + copy
    slots = near * far * cap
    hit = iota((slots, rows), 0).astype(F32) == slot
    label = jnp.sum(jnp.where(hit, place + 1.0, 0.0), 1, keepdims=True)
    return jnp.where(hit, 1.0, 0.0).astype(BF16), label


def image_ids(lengths, group, rows, tokens):
    images = lengths.shape[1]
    square = (images, images)
    sizes = jnp.broadcast_to(lengths.astype(F32), square)
    row, col = iota(square, 0), iota(square, 1)
    sizes_down = jnp.sum(jnp.where(row == col, sizes, 0.0), 1, keepdims=True)
    ends_down = jnp.sum(jnp.where(col <= row, sizes, 0.0), 1, keepdims=True)
    ends_across = jnp.sum(jnp.where(row <= col, sizes_down, 0.0), 0, keepdims=True)
    base = group * rows
    own = (base + (iota((1, 4 * rows), 1) >> 2)).astype(F32)
    near = (base - rows + (iota((12 * rows, 1), 0) >> 2)).astype(F32)
    own_image = jnp.sum(jnp.where(ends_down <= own, 1.0, 0.0), 0, keepdims=True)
    near_image = jnp.sum(jnp.where(ends_across <= near, 1.0, 0.0), 1, keepdims=True)
    inside = (near >= 0.0) & (near < float(tokens))
    return own_image, jnp.where(inside, near_image, -1.0)


def kernel(
    sizes,
    grad_out,
    dest,
    w_down,
    pre_act,
    w_up,
    queries,
    keys,
    values,
    lengths,
    out_q,
    out_k,
    out_v,
    go,
    wd,
    wt,
    wu,
    pre,
    qs,
    kx,
    vx,
    dst,
    lens,
    part,
    part_in,
    near_out,
    near_in,
    far_out,
    far_in,
    mix,
    mix_in,
    back,
    back_in,
    probs,
    probs_low,
    pack,
    swap,
    spread,
    slopes,
    own_part,
    ready,
    load_sem,
    down_sem,
    part_s,
    part_r,
    halo_s,
    halo_r,
    near_s,
    near_r,
    far_s,
    far_r,
    mix_s,
    mix_r,
    back_s,
    back_r,
):
    sects, groups, spans, near, far, cap = sizes
    rows = grad_out.shape[0]
    hidden = w_up.shape[0]
    cols = queries.shape[0]
    patches = 4 * rows
    x, g, y = lax.axis_index("sect"), lax.axis_index("grp"), lax.axis_index("span")
    g_hi, g_lo = g // near, g % near

    def at_xy(dx, dy):
        return ((x + dx) % sects, g, (y + dy) % spans)

    def hops(pair):
        return min(pair[0], sects - pair[0]) + min(pair[1], spans - pair[1])

    others = [(dx, dy) for dx in range(sects) for dy in range(spans) if dx or dy]
    others.sort(key=hops, reverse=True)

    def at_y(d):
        return (x, g, (y + d) % spans)

    def at_near(d):
        return (x, g_hi * near + (g_lo + d) % near, y)

    def at_far(d):
        return (x, ((g_hi + d) % far) * near + g_lo, y)

    def at_g(d):
        return (x, (g + d + groups) % groups, y)

    sent = []

    def send(src, to, send_sem, recv_sem, peer):
        copy = pltpu.make_async_remote_copy(
            src_ref=src,
            dst_ref=to,
            send_sem=send_sem,
            recv_sem=recv_sem,
            device_id=peer,
            device_id_type=pl.DeviceIdType.MESH,
        )
        copy.start()
        sent.append(copy)
        return copy

    def load(src, to, sem):
        copy = pltpu.make_async_copy(src, to, sem)
        copy.start()
        return copy

    order_y = far_first(spans) + [0]
    load_go = load(grad_out, go, load_sem.at[0])
    load_dst = load(dest, dst, load_sem.at[1])
    load_wd = []
    load_k = load(keys, kx.at[1], load_sem.at[4])
    load_v = load(values, vx.at[1], load_sem.at[5])
    for d in order_y:
        chunk = pl.ds(pl.multiple_of(((y + d) % spans) * hidden, 16), hidden)
        load_wd.append(load(w_down.at[chunk, :], wd.at[chunk, :], down_sem.at[d]))
    load_len = load(lengths, lens, load_sem.at[2])
    load_q = load(queries, qs, load_sem.at[3])
    load_pre = load(pre_act, pre, load_sem.at[6])
    load_wt = load(w_up, wt, load_sem.at[7])

    barrier = pltpu.get_barrier_semaphore()
    far_steps = sorted({1 % far, far - 1})
    peers = [at_far(d) for d in far_steps]
    peers += [at_near(d) for d in range(1, near)]
    peers += [at_g(1), at_g(-1)]
    peers += [at_xy(dx, dy) for dx, dy in others]
    def signal(sem, peer):
        pl.semaphore_signal(sem, inc=1, device_id=peer, device_id_type=pl.DeviceIdType.MESH)

    for peer in peers:
        signal(barrier, peer)

    load_go.wait()
    part_copies = []
    for d, loaded in zip(order_y, load_wd):
        loaded.wait()
        chunk = pl.ds(pl.multiple_of(((y + d) % spans) * hidden, 16), hidden)
        product = dot(go[...], wd[chunk, :], LAST)
        if d == 0:
            own_part[...] = product
            continue
        part[d - 1] = product.astype(BF16)
        if not part_copies:
            pl.semaphore_wait(barrier, len(peers))
            for i, step in enumerate(far_steps):
                signal(ready.at[0, i], at_far(step))
        part_copies.append(
            send(part.at[d - 1], part_in.at[d - 1], part_s.at[d - 1], part_r.at[d - 1], at_y(d))
        )
    load_k.wait()
    load_v.wait()
    halo_copies = []
    for i, (full, step) in enumerate(((kx, 1), (vx, 1), (kx, -1), (vx, -1))):
        land = full.at[0 if step == 1 else 2]
        halo_copies.append(send(full.at[1], land, halo_s.at[i], halo_r.at[i], at_g(step)))
    load_dst.wait()
    pack[...], label = token_packing(dst[...], rows, near, far, cap)
    near_out[:, hidden:] = jnp.broadcast_to(label, (near * far * cap, LABEL_LANES)).astype(BF16)
    slots = near * far * cap
    near_rows, far_rows = far * cap, near * cap
    out_row = iota((slots, slots), 0)
    in_row = iota((slots, slots), 1)
    source = ((out_row >> log2(cap)) & (near - 1)) * near_rows
    source = source + (out_row >> log2(far_rows)) * cap + (out_row & (cap - 1))
    swap[...] = jnp.where(source == in_row, 1.0, 0.0).astype(BF16)
    for i in range(len(far_steps)):
        pl.semaphore_wait(ready.at[0, i], 1)
    second = [d for d in (1, far - 1, 2, far - 2) if far > 2 and d < far]
    second = sorted(set(second))
    for i, d in enumerate(second):
        signal(ready.at[1, i], at_far(d))

    total = own_part[...]
    for d, copy in zip(far_first(spans), part_copies):
        copy.wait_recv()
        total = total + part_in[d - 1].astype(F32)
    near_out[:, :hidden] = dot(pack[...], total.astype(BF16)).astype(BF16)
    near_copies = []
    for d in range(near - 1, 0, -1):
        block = pl.ds(pl.multiple_of(((g_lo + d) % near) * near_rows, near_rows), near_rows)
        near_copies.append(
            send(
                near_out.at[block, :],
                near_in.at[pl.ds(d * near_rows, near_rows), :],
                near_s.at[d - 1],
                near_r.at[d - 1],
                at_near(d),
            )
        )
    mine = pl.ds(pl.multiple_of(g_lo * near_rows, near_rows), near_rows)
    near_in[pl.ds(0, near_rows), :] = near_out[mine, :]
    for copy in near_copies:
        copy.wait_recv()
    far_out[...] = dot(swap[...], near_in[...]).astype(BF16)
    for i in range(len(second)):
        pl.semaphore_wait(ready.at[1, i], 1)
    far_copies = []

    def release(d):
        block = pl.ds(pl.multiple_of(((g_hi + d) % far) * far_rows, far_rows), far_rows)
        far_copies.append(
            send(
                far_out.at[block, :],
                far_in.at[pl.ds(d * far_rows, far_rows), :],
                far_s.at[d - 1],
                far_r.at[d - 1],
                at_far(d),
            )
        )
    waves = [[d for d in far_first(far) if min(d, far - d) == k] for k in range(far // 2, 0, -1)]
    waves += [[]] * (4 - len(waves))
    for d in waves[0] + waves[1]:
        release(d)
    mine = pl.ds(pl.multiple_of(g_hi * far_rows, far_rows), far_rows)
    far_in[pl.ds(0, far_rows), :] = far_out[mine, :]

    scale = HEAD_DIM ** (-0.5)
    width = 4 * cols
    load_q.wait()
    for copy in halo_copies:
        copy.wait_recv()
    load_len.wait()
    own_image, near_image = image_ids(lens[...], g, rows, rows * groups)
    top_score = None
    for block in range(3):
        scores = dot(kx[block], qs[...], FIRST) * scale
        image = near_image[block * patches : (block + 1) * patches]
        scores = jnp.where(image == own_image, scores, -jnp.inf)
        probs[block] = scores
        top = jnp.max(scores, 0, keepdims=True)
        top_score = top if top_score is None else jnp.maximum(top_score, top)
    weight_sum = jnp.zeros((1, patches), F32)
    for block in range(3):
        weights = jnp.exp(probs[block] - top_score)
        probs[block] = weights
        weight_sum = weight_sum + jnp.sum(weights, 0, keepdims=True)
    attended = jnp.zeros((cols, patches), F32)
    for block in range(3):
        weights = probs[block] / weight_sum
        probs[block] = weights
        probs_low[block] = weights.astype(BF16)
        attended = attended + dot(vx[block], probs_low[block])
    load_pre.wait()
    slopes[...] = gelu_slope(pre[...].astype(F32))
    token, patch = iota((rows, patches), 0), iota((rows, patches), 1)
    for p in range(4):
        spread[p] = jnp.where(patch == 4 * token + p, 1.0, 0.0).astype(BF16)
    load_wt.wait()
    step_rows = 32

    def regroup(i, carry):
        some = pl.ds(pl.multiple_of(i * step_rows, step_rows), step_rows)
        for d in range(sects * spans):
            for p in range(4):
                start = (p * sects * spans + d) * cols
                wu[d, some, p * cols : (p + 1) * cols] = wt[some, start : start + cols]
        return carry

    halves = hidden // step_rows // 2
    lax.fori_loop(0, halves, regroup, 0)
    for d in waves[2]:
        release(d)
    lax.fori_loop(halves, hidden // step_rows, regroup, 0)

    for d in waves[3]:
        release(d)

    for copy in far_copies:
        copy.wait_recv()
    arrived = far_in[...]
    place = arrived[:, hidden : hidden + 1].astype(F32)
    unpacker = jnp.where(place == (iota((slots, rows), 1) + 1).astype(F32), 1.0, 0.0)
    grad_hidden = dot(unpacker.astype(BF16), arrived[:, :hidden], FIRST)
    grad_pre = (grad_hidden * slopes[...]).astype(BF16)
    mix_copies = []
    for dx, dy in others:
        owner = ((x + dx) % sects) * spans + (y + dy) % spans
        i = dx * spans + dy - 1
        mix[i] = dot(grad_pre, wu[owner]).astype(BF16)
        mix_copies.append(
            (i, send(mix.at[i], mix_in.at[i], mix_s.at[i], mix_r.at[i], at_xy(dx, dy)))
        )
    share = dot(grad_pre, wu[x * spans + y])
    for i, copy in mix_copies:
        copy.wait_recv()
        share = share + mix_in[i].astype(F32)
    share = share.astype(BF16)
    grad_attn = jnp.zeros((cols, patches), F32)
    for p in range(4):
        grad_attn = grad_attn + dot(share[:, p * cols : (p + 1) * cols], spread[p], FIRST)
    row_delta = jnp.sum(grad_attn * attended, 0, keepdims=True)
    grad_attn = grad_attn.astype(BF16)
    back_copies = []
    q = qs[...]

    def give_back(block, kind, term):
        side = block // 2
        back[side, kind] = term.astype(BF16)
        back_copies.append(
            send(
                back.at[side, kind],
                back_in.at[1 - side, kind],
                back_s.at[side, kind],
                back_r.at[1 - side, kind],
                at_g(block - 1),
            )
        )

    def value_term(block):
        return dot(grad_attn, probs_low[block], LAST)

    def score_term(block):
        grad_probs = dot(vx[block], grad_attn, FIRST)
        return (probs[block] * (grad_probs - row_delta)).astype(BF16)

    for block in (0, 2):
        give_back(block, 1, value_term(block))
    grad_query = jnp.zeros((cols, patches), F32)
    for block in (0, 2):
        score_part = score_term(block)
        give_back(block, 0, dot(q, score_part, LAST) * scale)
        grad_query = grad_query + dot(kx[block], score_part)
    score_part = score_term(1)
    key_part = dot(q, score_part, LAST) * scale
    value_part = value_term(1)
    grad_query = grad_query + dot(kx[1], score_part)
    out_q[...] = (grad_query * scale).astype(BF16)
    for copy in back_copies:
        copy.wait_recv()
    for side in range(2):
        key_part = key_part + back_in[side, 0].astype(F32)
        value_part = value_part + back_in[side, 1].astype(F32)
    out_k[...] = key_part.astype(BF16)
    out_v[...] = value_part.astype(BF16)
    for copy in sent:
        copy.wait_send()


def move(*refs):
    half = len(refs) // 2
    for source, target in zip(refs[:half], refs[half:]):
        target[...] = source[...]


def on_device(
    grad_out, destination, w_down, pre_act, w_up, queries, key_states, value_states, lengths
):
    sects, groups, spans = (lax.axis_size(a) for a in ("sect", "grp", "span"))
    rows, merged = grad_out.shape
    merge_rows, hidden = w_up.shape
    cols = queries.shape[1]
    patches = 4 * rows
    near = 8 if groups % 8 == 0 and groups > 8 else 2
    far = groups // near
    cap = rows // min(groups, rows // 2)
    slots = groups * cap
    width = 4 * cols
    wide = hidden + LABEL_LANES
    dma = pltpu.SemaphoreType.DMA
    vmem = pltpu.VMEM
    some = pl.BlockSpec(memory_space=pl.ANY)
    out = jax.ShapeDtypeStruct((cols, patches), BF16)
    sizes = (sects, groups, spans, near, far, cap)
    outs = pl.pallas_call(
        functools.partial(kernel, sizes),
        out_shape=(out, out, out),
        in_specs=[some] * 9,
        out_specs=[pl.BlockSpec(memory_space=pltpu.VMEM)] * 3,
        scratch_shapes=[
            vmem((rows, merged), BF16),
            vmem(w_down.shape, BF16),
            vmem((hidden, merge_rows), BF16),
            vmem((sects * spans, hidden, width), BF16),
            vmem((rows, hidden), BF16),
            vmem((cols, patches), BF16),
            vmem((3, cols, patches), BF16),
            vmem((3, cols, patches), BF16),
            vmem((1, rows), jnp.int32),
            vmem((1, lengths.shape[0]), jnp.int32),
            vmem((spans - 1, rows, hidden), BF16),
            vmem((spans - 1, rows, hidden), BF16),
            vmem((slots, wide), BF16),
            vmem((slots, wide), BF16),
            vmem((slots, wide), BF16),
            vmem((slots, wide), BF16),
            vmem((sects * spans - 1, rows, width), BF16),
            vmem((sects * spans - 1, rows, width), BF16),
            vmem((2, 2, cols, patches), BF16),
            vmem((2, 2, cols, patches), BF16),
            vmem((3, patches, patches), F32),
            vmem((3, patches, patches), BF16),
            vmem((slots, rows), BF16),
            vmem((slots, slots), BF16),
            vmem((4, rows, patches), BF16),
            vmem((rows, hidden), F32),
            vmem((rows, hidden), F32),
            pltpu.SemaphoreType.REGULAR((2, 4)),
            dma((8,)),
            dma((spans,)),
            dma((spans - 1,)),
            dma((spans - 1,)),
            dma((4,)),
            dma((4,)),
            dma((near - 1,)),
            dma((near - 1,)),
            dma((far - 1,)),
            dma((far - 1,)),
            dma((sects * spans - 1,)),
            dma((sects * spans - 1,)),
            dma((2, 2)),
            dma((2, 2)),
        ],
        compiler_params=pltpu.CompilerParams(
            collective_id=0, has_side_effects=True, vmem_limit_bytes=60 * 1024 * 1024
        ),
        name="merger_attention_backward",
    )(
        grad_out,
        destination.reshape(1, rows),
        w_down,
        pre_act,
        w_up.T,
        queries.T,
        key_states.T,
        value_states.T,
        lengths.reshape(1, lengths.shape[0]),
    )
    outs = pl.pallas_call(
        move,
        out_shape=(out, out, out),
        in_specs=[pl.BlockSpec(memory_space=pltpu.VMEM)] * 3,
        out_specs=[pl.BlockSpec(memory_space=pltpu.VMEM)] * 3,
        name="gradients_out",
    )(*outs)
    return tuple(each.T for each in outs)


def solution(mesh):
    placed = (
        P("grp", "span"),
        P("grp"),
        P("sect", "span"),
        P("grp", ("sect", "span")),
        P(None, ("sect", "span")),
        P("grp", ("sect", "span")),
        P("grp", ("sect", "span")),
        P("grp", ("sect", "span")),
        P(),
    )
    return jax.shard_map(
        on_device,
        mesh=mesh,
        in_specs=placed,
        out_specs=(
            P("grp", ("sect", "span")),
            P("grp", ("sect", "span")),
            P("grp", ("sect", "span")),
        ),
        check_vma=False,
    )
```

```python
import functools

import jax
import jax.numpy as jnp
from jax import lax
from jax.experimental import pallas as pl
from jax.experimental.pallas import tpu as pltpu
from jax.sharding import PartitionSpec as P

HEAD_DIM = 80
LABEL_LANES = 64
BF16 = jnp.bfloat16
F32 = jnp.float32
LAST = (((1,), (1,)), ((), ()))
FIRST = (((0,), (0,)), ((), ()))


def dot(a, b, dims=(((1,), (0,)), ((), ()))):
    return lax.dot_general(a, b, dims, preferred_element_type=F32)


def iota(shape, dim):
    return lax.broadcasted_iota(jnp.int32, shape, dim)


def gelu_slope(values):
    normal_cdf = 0.5 * (1.0 + lax.erf(values * 0.7071067811865476))
    return normal_cdf + values * jnp.exp(-0.5 * values * values) * 0.3989422804014327


def log2(n):
    return n.bit_length() - 1


def far_first(n):
    return sorted(range(1, n), key=lambda d: -min(d, n - d))


def token_packing(dest, rows, near, far, cap):
    where_to = dest.astype(F32)
    group = jnp.floor((where_to + 0.5) * (1.0 / rows))
    place = where_to - group * rows
    square = (rows, rows)
    across = jnp.broadcast_to(group, square)
    down = jnp.sum(jnp.where(iota(square, 0) == iota(square, 1), across, 0.0), 1, keepdims=True)
    earlier = (down == across) & (iota(square, 0) < iota(square, 1))
    copy = jnp.sum(jnp.where(earlier, 1.0, 0.0), 0, keepdims=True)
    group_hi = jnp.floor((group + 0.5) * (1.0 / near))
    slot = (group - group_hi * near) * (far * cap) + group_hi * cap + copy
    slots = near * far * cap
    hit = iota((slots, rows), 0).astype(F32) == slot
    label = jnp.sum(jnp.where(hit, place + 1.0, 0.0), 1, keepdims=True)
    return jnp.where(hit, 1.0, 0.0).astype(BF16), label


def image_ids(lengths, group, rows, tokens):
    images = lengths.shape[1]
    square = (images, images)
    sizes = jnp.broadcast_to(lengths.astype(F32), square)
    row, col = iota(square, 0), iota(square, 1)
    sizes_down = jnp.sum(jnp.where(row == col, sizes, 0.0), 1, keepdims=True)
    ends_down = jnp.sum(jnp.where(col <= row, sizes, 0.0), 1, keepdims=True)
    ends_across = jnp.sum(jnp.where(row <= col, sizes_down, 0.0), 0, keepdims=True)
    base = group * rows
    own = (base + (iota((1, 4 * rows), 1) >> 2)).astype(F32)
    near = (base - rows + (iota((12 * rows, 1), 0) >> 2)).astype(F32)
    own_image = jnp.sum(jnp.where(ends_down <= own, 1.0, 0.0), 0, keepdims=True)
    near_image = jnp.sum(jnp.where(ends_across <= near, 1.0, 0.0), 1, keepdims=True)
    inside = (near >= 0.0) & (near < float(tokens))
    return own_image, jnp.where(inside, near_image, -1.0)


def kernel(
    sizes,
    grad_out,
    dest,
    w_down,
    pre_act,
    w_up,
    queries,
    keys,
    values,
    lengths,
    out_q,
    out_k,
    out_v,
    go,
    wd,
    wt,
    wu,
    pre,
    qs,
    kx,
    vx,
    dst,
    lens,
    part,
    part_in,
    near_out,
    near_in,
    far_out,
    far_in,
    mix,
    mix_a,
    mix_b,
    fin_a,
    fin_b,
    sum_a,
    sum_b,
    back,
    back_in,
    probs,
    probs_low,
    pack,
    swap,
    spread,
    slopes,
    own_part,
    ready,
    load_sem,
    down_sem,
    part_s,
    part_r,
    halo_s,
    halo_r,
    near_s,
    near_r,
    far_s,
    far_r,
    a1_s,
    a1_r,
    b1_s,
    b1_r,
    a2_s,
    a2_r,
    b2_s,
    b2_r,
    back_s,
    back_r,
):
    sects, groups, spans, near, far, cap, split = sizes
    rows = grad_out.shape[0]
    hidden = w_up.shape[0]
    cols = queries.shape[0]
    patches = 4 * rows
    x, g, y = lax.axis_index("sect"), lax.axis_index("grp"), lax.axis_index("span")
    g_hi, g_lo = g // near, g % near

    def at_x(d):
        return ((x + d) % sects, g, y)

    def at_y(d):
        return (x, g, (y + d) % spans)

    def at_near(d):
        return (x, g_hi * near + (g_lo + d) % near, y)

    def at_far(d):
        return (x, ((g_hi + d) % far) * near + g_lo, y)

    def at_g(d):
        return (x, (g + d + groups) % groups, y)

    sent = []

    def send(src, to, send_sem, recv_sem, peer):
        copy = pltpu.make_async_remote_copy(
            src_ref=src,
            dst_ref=to,
            send_sem=send_sem,
            recv_sem=recv_sem,
            device_id=peer,
            device_id_type=pl.DeviceIdType.MESH,
        )
        copy.start()
        sent.append(copy)
        return copy

    def load(src, to, sem):
        copy = pltpu.make_async_copy(src, to, sem)
        copy.start()
        return copy

    order_y = far_first(spans) + [0]
    load_go = load(grad_out, go, load_sem.at[0])
    load_dst = load(dest, dst, load_sem.at[1])
    load_wd = []
    load_k = load(keys, kx.at[1], load_sem.at[4])
    load_v = load(values, vx.at[1], load_sem.at[5])
    for d in order_y:
        chunk = pl.ds(pl.multiple_of(((y + d) % spans) * hidden, 16), hidden)
        load_wd.append(load(w_down.at[chunk, :], wd.at[chunk, :], down_sem.at[d]))
    load_len = load(lengths, lens, load_sem.at[2])
    load_q = load(queries, qs, load_sem.at[3])
    load_pre = load(pre_act, pre, load_sem.at[6])
    load_wt = load(w_up, wt, load_sem.at[7])

    barrier = pltpu.get_barrier_semaphore()
    far_steps = sorted({1 % far, far - 1})
    peers = [at_far(d) for d in far_steps]
    peers += [at_y(d) for d in range(1, spans)]
    peers += [at_near(d) for d in range(1, near)]
    peers += [at_g(1), at_g(-1)]
    peers += [at_x(d) for d in range(1, sects)]
    def signal(sem, peer):
        pl.semaphore_signal(sem, inc=1, device_id=peer, device_id_type=pl.DeviceIdType.MESH)

    for peer in peers:
        signal(barrier, peer)

    load_go.wait()
    part_copies = []
    for d, loaded in zip(order_y, load_wd):
        loaded.wait()
        chunk = pl.ds(pl.multiple_of(((y + d) % spans) * hidden, 16), hidden)
        product = dot(go[...], wd[chunk, :], LAST)
        if d == 0:
            own_part[...] = product
            continue
        part[d - 1] = product.astype(BF16)
        if not part_copies:
            pl.semaphore_wait(barrier, len(peers))
            for i, step in enumerate(far_steps):
                signal(ready.at[0, i], at_far(step))
        part_copies.append(
            send(part.at[d - 1], part_in.at[d - 1], part_s.at[d - 1], part_r.at[d - 1], at_y(d))
        )
    load_k.wait()
    load_v.wait()
    halo_copies = []
    for i, (full, step) in enumerate(((kx, 1), (vx, 1), (kx, -1), (vx, -1))):
        land = full.at[0 if step == 1 else 2]
        halo_copies.append(send(full.at[1], land, halo_s.at[i], halo_r.at[i], at_g(step)))
    load_dst.wait()
    pack[...], label = token_packing(dst[...], rows, near, far, cap)
    near_out[:, hidden:] = jnp.broadcast_to(label, (near * far * cap, LABEL_LANES)).astype(BF16)
    slots = near * far * cap
    near_rows, far_rows = far * cap, near * cap
    out_row = iota((slots, slots), 0)
    in_row = iota((slots, slots), 1)
    source = ((out_row >> log2(cap)) & (near - 1)) * near_rows
    source = source + (out_row >> log2(far_rows)) * cap + (out_row & (cap - 1))
    swap[...] = jnp.where(source == in_row, 1.0, 0.0).astype(BF16)
    for i in range(len(far_steps)):
        pl.semaphore_wait(ready.at[0, i], 1)
    second = [d for d in (1, far - 1, 2, far - 2) if far > 2 and d < far]
    second = sorted(set(second))
    for i, d in enumerate(second):
        signal(ready.at[1, i], at_far(d))

    total = own_part[...]
    for d, copy in zip(far_first(spans), part_copies):
        copy.wait_recv()
        total = total + part_in[d - 1].astype(F32)
    near_out[:, :hidden] = dot(pack[...], total.astype(BF16)).astype(BF16)
    near_copies = []
    for d in range(near - 1, 0, -1):
        block = pl.ds(pl.multiple_of(((g_lo + d) % near) * near_rows, near_rows), near_rows)
        near_copies.append(
            send(
                near_out.at[block, :],
                near_in.at[pl.ds(d * near_rows, near_rows), :],
                near_s.at[d - 1],
                near_r.at[d - 1],
                at_near(d),
            )
        )
    mine = pl.ds(pl.multiple_of(g_lo * near_rows, near_rows), near_rows)
    near_in[pl.ds(0, near_rows), :] = near_out[mine, :]
    for copy in near_copies:
        copy.wait_recv()
    far_out[...] = dot(swap[...], near_in[...]).astype(BF16)
    for i in range(len(second)):
        pl.semaphore_wait(ready.at[1, i], 1)
    far_copies = []

    def release(d):
        block = pl.ds(pl.multiple_of(((g_hi + d) % far) * far_rows, far_rows), far_rows)
        far_copies.append(
            send(
                far_out.at[block, :],
                far_in.at[pl.ds(d * far_rows, far_rows), :],
                far_s.at[d - 1],
                far_r.at[d - 1],
                at_far(d),
            )
        )
    waves = [[d for d in far_first(far) if min(d, far - d) == k] for k in range(far // 2, 0, -1)]
    waves += [[]] * (4 - len(waves))
    for d in waves[0] + waves[1]:
        release(d)
    mine = pl.ds(pl.multiple_of(g_hi * far_rows, far_rows), far_rows)
    far_in[pl.ds(0, far_rows), :] = far_out[mine, :]

    scale = HEAD_DIM ** (-0.5)
    width = 4 * cols
    load_q.wait()
    for copy in halo_copies:
        copy.wait_recv()
    load_len.wait()
    own_image, near_image = image_ids(lens[...], g, rows, rows * groups)
    top_score = None
    for block in range(3):
        scores = dot(kx[block], qs[...], FIRST) * scale
        image = near_image[block * patches : (block + 1) * patches]
        scores = jnp.where(image == own_image, scores, -jnp.inf)
        probs[block] = scores
        top = jnp.max(scores, 0, keepdims=True)
        top_score = top if top_score is None else jnp.maximum(top_score, top)
    weight_sum = jnp.zeros((1, patches), F32)
    for block in range(3):
        weights = jnp.exp(probs[block] - top_score)
        probs[block] = weights
        weight_sum = weight_sum + jnp.sum(weights, 0, keepdims=True)
    attended = jnp.zeros((cols, patches), F32)
    for block in range(3):
        weights = probs[block] / weight_sum
        probs[block] = weights
        probs_low[block] = weights.astype(BF16)
        attended = attended + dot(vx[block], probs_low[block])
    load_pre.wait()
    slopes[...] = gelu_slope(pre[...].astype(F32))
    token, patch = iota((rows, patches), 0), iota((rows, patches), 1)
    for p in range(4):
        spread[p] = jnp.where(patch == 4 * token + p, 1.0, 0.0).astype(BF16)
    load_wt.wait()
    step_rows = 32

    def regroup(i, carry):
        some = pl.ds(pl.multiple_of(i * step_rows, step_rows), step_rows)
        for d in range(sects * spans):
            for p in range(4):
                start = (p * sects * spans + d) * cols
                wu[d, some, p * cols : (p + 1) * cols] = wt[some, start : start + cols]
        return carry

    halves = hidden // step_rows // 2
    lax.fori_loop(0, halves, regroup, 0)
    for d in waves[2]:
        release(d)
    lax.fori_loop(halves, hidden // step_rows, regroup, 0)

    for d in waves[3]:
        release(d)

    for copy in far_copies:
        copy.wait_recv()
    arrived = far_in[...]
    place = arrived[:, hidden : hidden + 1].astype(F32)
    unpacker = jnp.where(place == (iota((slots, rows), 1) + 1).astype(F32), 1.0, 0.0)
    grad_hidden = dot(unpacker.astype(BF16), arrived[:, :hidden], FIRST)
    grad_pre = (grad_hidden * slopes[...]).astype(BF16)
    top, low = pl.ds(0, split), pl.ds(split, rows - split)
    a_copies, b_copies = {}, {}
    pairs = [(dx, dy) for dx in far_first(sects) for dy in far_first(spans)]
    pairs.sort(key=lambda d: -min(d[0], sects - d[0]) - min(d[1], spans - d[1]))
    pairs += [(dx, 0) for dx in far_first(sects)] + [(0, dy) for dy in far_first(spans)]
    for dx, dy in pairs + [(0, 0)]:
        owner = ((x + dx) % sects) * spans + (y + dy) % spans
        mix[dx, dy] = dot(grad_pre, wu[owner]).astype(BF16)
        if dx:
            a_copies[dx, dy] = send(
                mix.at[dx, dy, top, :],
                mix_a.at[dx - 1, dy],
                a1_s.at[dx - 1, dy],
                a1_r.at[dx - 1, dy],
                at_x(dx),
            )
        if dy:
            b_copies[dx, dy] = send(
                mix.at[dx, dy, low, :],
                mix_b.at[dy - 1, dx],
                b1_s.at[dy - 1, dx],
                b1_r.at[dy - 1, dx],
                at_y(dy),
            )
    a2_copies, b2_copies = [], []

    def sum_top(dy):
        total = mix[0, dy, top, :].astype(F32)
        for dx in far_first(sects):
            a_copies[dx, dy].wait_recv()
            total = total + mix_a[dx - 1, dy].astype(F32)
        return total

    def sum_low(dx):
        total = mix[dx, 0, low, :].astype(F32)
        for dy in far_first(spans):
            b_copies[dx, dy].wait_recv()
            total = total + mix_b[dy - 1, dx].astype(F32)
        return total

    for i in range(max(sects, spans) - 1):
        if i < sects - 1:
            d = far_first(sects)[i]
            sum_b[d - 1] = sum_low(d).astype(BF16)
            b2_copies.append(
                send(sum_b.at[d - 1], fin_b.at[d - 1], b2_s.at[d - 1], b2_r.at[d - 1], at_x(d))
            )
        if i < spans - 1:
            d = far_first(spans)[i]
            sum_a[d - 1] = sum_top(d).astype(BF16)
            a2_copies.append(
                send(sum_a.at[d - 1], fin_a.at[d - 1], a2_s.at[d - 1], a2_r.at[d - 1], at_y(d))
            )
    share_b, share_a = sum_low(0), sum_top(0)
    for copy in a2_copies + b2_copies:
        copy.wait_recv()
    for d in range(spans - 1):
        share_a = share_a + fin_a[d].astype(F32)
    for d in range(sects - 1):
        share_b = share_b + fin_b[d].astype(F32)
    share = jnp.concatenate([share_a, share_b], 0).astype(BF16)

    grad_attn = jnp.zeros((cols, patches), F32)
    for p in range(4):
        grad_attn = grad_attn + dot(share[:, p * cols : (p + 1) * cols], spread[p], FIRST)
    row_delta = jnp.sum(grad_attn * attended, 0, keepdims=True)
    grad_attn = grad_attn.astype(BF16)
    back_copies = []
    q = qs[...]

    def give_back(block, kind, term):
        side = block // 2
        back[side, kind] = term.astype(BF16)
        back_copies.append(
            send(
                back.at[side, kind],
                back_in.at[1 - side, kind],
                back_s.at[side, kind],
                back_r.at[1 - side, kind],
                at_g(block - 1),
            )
        )

    def value_term(block):
        return dot(grad_attn, probs_low[block], LAST)

    def score_term(block):
        grad_probs = dot(vx[block], grad_attn, FIRST)
        return (probs[block] * (grad_probs - row_delta)).astype(BF16)

    for block in (0, 2):
        give_back(block, 1, value_term(block))
    grad_query = jnp.zeros((cols, patches), F32)
    for block in (0, 2):
        score_part = score_term(block)
        give_back(block, 0, dot(q, score_part, LAST) * scale)
        grad_query = grad_query + dot(kx[block], score_part)
    score_part = score_term(1)
    key_part = dot(q, score_part, LAST) * scale
    value_part = value_term(1)
    grad_query = grad_query + dot(kx[1], score_part)
    out_q[...] = (grad_query * scale).astype(BF16)
    for copy in back_copies:
        copy.wait_recv()
    for side in range(2):
        key_part = key_part + back_in[side, 0].astype(F32)
        value_part = value_part + back_in[side, 1].astype(F32)
    out_k[...] = key_part.astype(BF16)
    out_v[...] = value_part.astype(BF16)
    for copy in sent:
        copy.wait_send()


def move(*refs):
    half = len(refs) // 2
    for source, target in zip(refs[:half], refs[half:]):
        target[...] = source[...]


def on_device(
    grad_out, destination, w_down, pre_act, w_up, queries, key_states, value_states, lengths
):
    sects, groups, spans = (lax.axis_size(a) for a in ("sect", "grp", "span"))
    rows, merged = grad_out.shape
    merge_rows, hidden = w_up.shape
    cols = queries.shape[1]
    patches = 4 * rows
    near = 8 if groups % 8 == 0 and groups > 8 else 2
    far = groups // near
    cap = rows // min(groups, rows // 2)
    slots = groups * cap
    split = (rows * 5 // 8 // 16) * 16 if rows >= 32 else rows // 2
    width = 4 * cols
    wide = hidden + LABEL_LANES
    dma = pltpu.SemaphoreType.DMA
    vmem = pltpu.VMEM
    some = pl.BlockSpec(memory_space=pl.ANY)
    out = jax.ShapeDtypeStruct((cols, patches), BF16)
    sizes = (sects, groups, spans, near, far, cap, split)
    outs = pl.pallas_call(
        functools.partial(kernel, sizes),
        out_shape=(out, out, out),
        in_specs=[some] * 9,
        out_specs=[pl.BlockSpec(memory_space=pltpu.VMEM)] * 3,
        scratch_shapes=[
            vmem((rows, merged), BF16),
            vmem(w_down.shape, BF16),
            vmem((hidden, merge_rows), BF16),
            vmem((sects * spans, hidden, width), BF16),
            vmem((rows, hidden), BF16),
            vmem((cols, patches), BF16),
            vmem((3, cols, patches), BF16),
            vmem((3, cols, patches), BF16),
            vmem((1, rows), jnp.int32),
            vmem((1, lengths.shape[0]), jnp.int32),
            vmem((spans - 1, rows, hidden), BF16),
            vmem((spans - 1, rows, hidden), BF16),
            vmem((slots, wide), BF16),
            vmem((slots, wide), BF16),
            vmem((slots, wide), BF16),
            vmem((slots, wide), BF16),
            vmem((sects, spans, rows, width), BF16),
            vmem((sects - 1, spans, split, width), BF16),
            vmem((spans - 1, sects, rows - split, width), BF16),
            vmem((spans - 1, split, width), BF16),
            vmem((sects - 1, rows - split, width), BF16),
            vmem((spans - 1, split, width), BF16),
            vmem((sects - 1, rows - split, width), BF16),
            vmem((2, 2, cols, patches), BF16),
            vmem((2, 2, cols, patches), BF16),
            vmem((3, patches, patches), F32),
            vmem((3, patches, patches), BF16),
            vmem((slots, rows), BF16),
            vmem((slots, slots), BF16),
            vmem((4, rows, patches), BF16),
            vmem((rows, hidden), F32),
            vmem((rows, hidden), F32),
            pltpu.SemaphoreType.REGULAR((2, 4)),
            dma((8,)),
            dma((spans,)),
            dma((spans - 1,)),
            dma((spans - 1,)),
            dma((4,)),
            dma((4,)),
            dma((near - 1,)),
            dma((near - 1,)),
            dma((far - 1,)),
            dma((far - 1,)),
            dma((sects - 1, spans)),
            dma((sects - 1, spans)),
            dma((spans - 1, sects)),
            dma((spans - 1, sects)),
            dma((spans - 1,)),
            dma((spans - 1,)),
            dma((sects - 1,)),
            dma((sects - 1,)),
            dma((2, 2)),
            dma((2, 2)),
        ],
        compiler_params=pltpu.CompilerParams(
            collective_id=0, has_side_effects=True, vmem_limit_bytes=60 * 1024 * 1024
        ),
        name="merger_attention_backward",
    )(
        grad_out,
        destination.reshape(1, rows),
        w_down,
        pre_act,
        w_up.T,
        queries.T,
        key_states.T,
        value_states.T,
        lengths.reshape(1, lengths.shape[0]),
    )
    outs = pl.pallas_call(
        move,
        out_shape=(out, out, out),
        in_specs=[pl.BlockSpec(memory_space=pltpu.VMEM)] * 3,
        out_specs=[pl.BlockSpec(memory_space=pltpu.VMEM)] * 3,
        name="gradients_out",
    )(*outs)
    return tuple(each.T for each in outs)


def solution(mesh):
    placed = (
        P("grp", "span"),
        P("grp"),
        P("sect", "span"),
        P("grp", ("sect", "span")),
        P(None, ("sect", "span")),
        P("grp", ("sect", "span")),
        P("grp", ("sect", "span")),
        P("grp", ("sect", "span")),
        P(),
    )
    return jax.shard_map(
        on_device,
        mesh=mesh,
        in_specs=placed,
        out_specs=(
            P("grp", ("sect", "span")),
            P("grp", ("sect", "span")),
            P("grp", ("sect", "span")),
        ),
        check_vma=False,
    )
```

```python
import functools

import jax
import jax.numpy as jnp
from jax import lax
from jax.experimental import pallas as pl
from jax.experimental.pallas import tpu as pltpu
from jax.sharding import PartitionSpec as P

HEAD_DIM = 80
LABEL_LANES = 64
BF16 = jnp.bfloat16
F32 = jnp.float32
LAST = (((1,), (1,)), ((), ()))
FIRST = (((0,), (0,)), ((), ()))


def dot(a, b, dims=(((1,), (0,)), ((), ()))):
    return lax.dot_general(a, b, dims, preferred_element_type=F32)


def iota(shape, dim):
    return lax.broadcasted_iota(jnp.int32, shape, dim)


def gelu_slope(values):
    normal_cdf = 0.5 * (1.0 + lax.erf(values * 0.7071067811865476))
    return normal_cdf + values * jnp.exp(-0.5 * values * values) * 0.3989422804014327


def log2(n):
    return n.bit_length() - 1


def far_first(n):
    return sorted(range(1, n), key=lambda d: -min(d, n - d))


def token_packing(dest, rows, near, far, cap):
    where_to = dest.astype(F32)
    group = jnp.floor((where_to + 0.5) * (1.0 / rows))
    place = where_to - group * rows
    square = (rows, rows)
    across = jnp.broadcast_to(group, square)
    down = jnp.sum(jnp.where(iota(square, 0) == iota(square, 1), across, 0.0), 1, keepdims=True)
    earlier = (down == across) & (iota(square, 0) < iota(square, 1))
    copy = jnp.sum(jnp.where(earlier, 1.0, 0.0), 0, keepdims=True)
    group_hi = jnp.floor((group + 0.5) * (1.0 / near))
    slot = (group - group_hi * near) * (far * cap) + group_hi * cap + copy
    slots = near * far * cap
    hit = iota((slots, rows), 0).astype(F32) == slot
    label = jnp.sum(jnp.where(hit, place + 1.0, 0.0), 1, keepdims=True)
    return jnp.where(hit, 1.0, 0.0).astype(BF16), label


def image_ids(lengths, group, rows, tokens):
    images = lengths.shape[1]
    square = (images, images)
    sizes = jnp.broadcast_to(lengths.astype(F32), square)
    row, col = iota(square, 0), iota(square, 1)
    sizes_down = jnp.sum(jnp.where(row == col, sizes, 0.0), 1, keepdims=True)
    ends_down = jnp.sum(jnp.where(col <= row, sizes, 0.0), 1, keepdims=True)
    ends_across = jnp.sum(jnp.where(row <= col, sizes_down, 0.0), 0, keepdims=True)
    base = group * rows
    own = (base + (iota((1, 4 * rows), 1) >> 2)).astype(F32)
    near = (base - rows + (iota((12 * rows, 1), 0) >> 2)).astype(F32)
    own_image = jnp.sum(jnp.where(ends_down <= own, 1.0, 0.0), 0, keepdims=True)
    near_image = jnp.sum(jnp.where(ends_across <= near, 1.0, 0.0), 1, keepdims=True)
    inside = (near >= 0.0) & (near < float(tokens))
    return own_image, jnp.where(inside, near_image, -1.0)


def kernel(
    sizes,
    grad_out,
    dest,
    w_down,
    pre_act,
    w_up,
    queries,
    keys,
    values,
    lengths,
    out_q,
    out_k,
    out_v,
    go,
    wd,
    wt,
    wu,
    pre,
    qs,
    kx,
    vx,
    dst,
    lens,
    part,
    part_in,
    near_out,
    near_in,
    far_out,
    far_in,
    mix,
    mix_a,
    mix_b,
    fin_a,
    fin_b,
    sum_a,
    sum_b,
    back,
    back_in,
    probs,
    probs_low,
    pack,
    swap,
    spread,
    slopes,
    own_part,
    ready,
    load_sem,
    down_sem,
    part_s,
    part_r,
    halo_s,
    halo_r,
    near_s,
    near_r,
    far_s,
    far_r,
    a1_s,
    a1_r,
    b1_s,
    b1_r,
    a2_s,
    a2_r,
    b2_s,
    b2_r,
    back_s,
    back_r,
):
    sects, groups, spans, near, far, cap, split = sizes
    rows = grad_out.shape[0]
    hidden = w_up.shape[0]
    cols = queries.shape[0]
    patches = 4 * rows
    x, g, y = lax.axis_index("sect"), lax.axis_index("grp"), lax.axis_index("span")
    g_hi, g_lo = g // near, g % near

    def at_x(d):
        return ((x + d) % sects, g, y)

    def at_y(d):
        return (x, g, (y + d) % spans)

    def at_near(d):
        return (x, g_hi * near + (g_lo + d) % near, y)

    def at_far(d):
        return (x, ((g_hi + d) % far) * near + g_lo, y)

    def at_g(d):
        return (x, (g + d + groups) % groups, y)

    sent = []

    def send(src, to, send_sem, recv_sem, peer):
        copy = pltpu.make_async_remote_copy(
            src_ref=src,
            dst_ref=to,
            send_sem=send_sem,
            recv_sem=recv_sem,
            device_id=peer,
            device_id_type=pl.DeviceIdType.MESH,
        )
        copy.start()
        sent.append(copy)
        return copy

    def load(src, to, sem):
        copy = pltpu.make_async_copy(src, to, sem)
        copy.start()
        return copy

    order_y = far_first(spans) + [0]
    load_go = load(grad_out, go, load_sem.at[0])
    load_dst = load(dest, dst, load_sem.at[1])
    load_wd = []
    load_k = load(keys, kx.at[1], load_sem.at[4])
    load_v = load(values, vx.at[1], load_sem.at[5])
    for d in order_y:
        chunk = pl.ds(pl.multiple_of(((y + d) % spans) * hidden, 16), hidden)
        load_wd.append(load(w_down.at[chunk, :], wd.at[chunk, :], down_sem.at[d]))
    load_len = load(lengths, lens, load_sem.at[2])
    load_q = load(queries, qs, load_sem.at[3])
    load_pre = load(pre_act, pre, load_sem.at[6])

    barrier = pltpu.get_barrier_semaphore()
    far_steps = sorted({1 % far, far - 1})
    peers = [at_far(d) for d in far_steps]
    peers += [at_y(d) for d in range(1, spans)]
    peers += [at_near(d) for d in range(1, near)]
    peers += [at_g(1), at_g(-1)]
    peers += [at_x(d) for d in range(1, sects)]
    def signal(sem, peer):
        pl.semaphore_signal(sem, inc=1, device_id=peer, device_id_type=pl.DeviceIdType.MESH)

    for peer in peers:
        signal(barrier, peer)

    load_go.wait()
    part_copies = []
    for d, loaded in zip(order_y, load_wd):
        loaded.wait()
        chunk = pl.ds(pl.multiple_of(((y + d) % spans) * hidden, 16), hidden)
        product = dot(go[...], wd[chunk, :], LAST)
        if d == 0:
            own_part[...] = product
            continue
        part[d - 1] = product.astype(BF16)
        if not part_copies:
            pl.semaphore_wait(barrier, len(peers))
            for i, step in enumerate(far_steps):
                signal(ready.at[0, i], at_far(step))
        part_copies.append(
            send(part.at[d - 1], part_in.at[d - 1], part_s.at[d - 1], part_r.at[d - 1], at_y(d))
        )
    load_wt = load(w_up, wt, load_sem.at[7])
    load_k.wait()
    load_v.wait()
    halo_copies = []
    for i, (full, step) in enumerate(((kx, 1), (vx, 1), (kx, -1), (vx, -1))):
        land = full.at[0 if step == 1 else 2]
        halo_copies.append(send(full.at[1], land, halo_s.at[i], halo_r.at[i], at_g(step)))
    load_dst.wait()
    pack[...], label = token_packing(dst[...], rows, near, far, cap)
    near_out[:, hidden:] = jnp.broadcast_to(label, (near * far * cap, LABEL_LANES)).astype(BF16)
    slots = near * far * cap
    near_rows, far_rows = far * cap, near * cap
    out_row = iota((slots, slots), 0)
    in_row = iota((slots, slots), 1)
    source = ((out_row >> log2(cap)) & (near - 1)) * near_rows
    source = source + (out_row >> log2(far_rows)) * cap + (out_row & (cap - 1))
    swap[...] = jnp.where(source == in_row, 1.0, 0.0).astype(BF16)
    for i in range(len(far_steps)):
        pl.semaphore_wait(ready.at[0, i], 1)
    second = [d for d in (1, far - 1, 2, far - 2) if far > 2 and d < far]
    second = sorted(set(second))
    for i, d in enumerate(second):
        signal(ready.at[1, i], at_far(d))

    total = own_part[...]
    for d, copy in zip(far_first(spans), part_copies):
        copy.wait_recv()
        total = total + part_in[d - 1].astype(F32)
    near_out[:, :hidden] = dot(pack[...], total.astype(BF16)).astype(BF16)
    near_copies = []
    for d in range(near - 1, 0, -1):
        block = pl.ds(pl.multiple_of(((g_lo + d) % near) * near_rows, near_rows), near_rows)
        near_copies.append(
            send(
                near_out.at[block, :],
                near_in.at[pl.ds(d * near_rows, near_rows), :],
                near_s.at[d - 1],
                near_r.at[d - 1],
                at_near(d),
            )
        )
    mine = pl.ds(pl.multiple_of(g_lo * near_rows, near_rows), near_rows)
    near_in[pl.ds(0, near_rows), :] = near_out[mine, :]
    for copy in near_copies:
        copy.wait_recv()
    far_out[...] = dot(swap[...], near_in[...]).astype(BF16)
    for i in range(len(second)):
        pl.semaphore_wait(ready.at[1, i], 1)
    far_copies = []

    def release(d):
        block = pl.ds(pl.multiple_of(((g_hi + d) % far) * far_rows, far_rows), far_rows)
        far_copies.append(
            send(
                far_out.at[block, :],
                far_in.at[pl.ds(d * far_rows, far_rows), :],
                far_s.at[d - 1],
                far_r.at[d - 1],
                at_far(d),
            )
        )
    waves = [[d for d in far_first(far) if min(d, far - d) == k] for k in range(far // 2, 0, -1)]
    waves += [[]] * (4 - len(waves))
    for d in waves[0] + waves[1]:
        release(d)
    mine = pl.ds(pl.multiple_of(g_hi * far_rows, far_rows), far_rows)
    far_in[pl.ds(0, far_rows), :] = far_out[mine, :]

    scale = HEAD_DIM ** (-0.5)
    width = 4 * cols
    load_q.wait()
    for copy in halo_copies:
        copy.wait_recv()
    load_len.wait()
    own_image, near_image = image_ids(lens[...], g, rows, rows * groups)
    top_score = None
    for block in range(3):
        scores = dot(kx[block], qs[...], FIRST) * scale
        image = near_image[block * patches : (block + 1) * patches]
        scores = jnp.where(image == own_image, scores, -jnp.inf)
        probs[block] = scores
        top = jnp.max(scores, 0, keepdims=True)
        top_score = top if top_score is None else jnp.maximum(top_score, top)
    weight_sum = jnp.zeros((1, patches), F32)
    for block in range(3):
        weights = jnp.exp(probs[block] - top_score)
        probs[block] = weights
        weight_sum = weight_sum + jnp.sum(weights, 0, keepdims=True)
    attended = jnp.zeros((cols, patches), F32)
    for block in range(3):
        weights = probs[block] / weight_sum
        probs[block] = weights
        probs_low[block] = weights.astype(BF16)
        attended = attended + dot(vx[block], probs_low[block])
    load_pre.wait()
    slopes[...] = gelu_slope(pre[...].astype(F32))
    token, patch = iota((rows, patches), 0), iota((rows, patches), 1)
    for p in range(4):
        spread[p] = jnp.where(patch == 4 * token + p, 1.0, 0.0).astype(BF16)
    load_wt.wait()
    step_rows = 32

    def regroup(i, carry):
        some = pl.ds(pl.multiple_of(i * step_rows, step_rows), step_rows)
        for d in range(sects * spans):
            for p in range(4):
                start = (p * sects * spans + d) * cols
                wu[d, some, p * cols : (p + 1) * cols] = wt[some, start : start + cols]
        return carry

    halves = hidden // step_rows // 2
    lax.fori_loop(0, halves, regroup, 0)
    for d in waves[2]:
        release(d)
    lax.fori_loop(halves, hidden // step_rows, regroup, 0)

    for d in waves[3]:
        release(d)

    for copy in far_copies:
        copy.wait_recv()
    arrived = far_in[...]
    place = arrived[:, hidden : hidden + 1].astype(F32)
    unpacker = jnp.where(place == (iota((slots, rows), 1) + 1).astype(F32), 1.0, 0.0)
    grad_hidden = dot(unpacker.astype(BF16), arrived[:, :hidden], FIRST)
    grad_pre = (grad_hidden * slopes[...]).astype(BF16)
    top, low = pl.ds(0, split), pl.ds(split, rows - split)
    a_copies, b_copies = {}, {}
    pairs = [(dx, dy) for dx in far_first(sects) for dy in far_first(spans)]
    pairs.sort(key=lambda d: -min(d[0], sects - d[0]) - min(d[1], spans - d[1]))
    pairs += [(dx, 0) for dx in far_first(sects)] + [(0, dy) for dy in far_first(spans)]
    for dx, dy in pairs + [(0, 0)]:
        owner = ((x + dx) % sects) * spans + (y + dy) % spans
        mix[dx, dy] = dot(grad_pre, wu[owner]).astype(BF16)
        if dx:
            a_copies[dx, dy] = send(
                mix.at[dx, dy, top, :],
                mix_a.at[dx - 1, dy],
                a1_s.at[dx - 1, dy],
                a1_r.at[dx - 1, dy],
                at_x(dx),
            )
        if dy:
            b_copies[dx, dy] = send(
                mix.at[dx, dy, low, :],
                mix_b.at[dy - 1, dx],
                b1_s.at[dy - 1, dx],
                b1_r.at[dy - 1, dx],
                at_y(dy),
            )
    a2_copies, b2_copies = [], []

    def sum_top(dy):
        total = mix[0, dy, top, :].astype(F32)
        for dx in far_first(sects):
            a_copies[dx, dy].wait_recv()
            total = total + mix_a[dx - 1, dy].astype(F32)
        return total

    def sum_low(dx):
        total = mix[dx, 0, low, :].astype(F32)
        for dy in far_first(spans):
            b_copies[dx, dy].wait_recv()
            total = total + mix_b[dy - 1, dx].astype(F32)
        return total

    for i in range(max(sects, spans) - 1):
        if i < sects - 1:
            d = far_first(sects)[i]
            sum_b[d - 1] = sum_low(d).astype(BF16)
            b2_copies.append(
                send(sum_b.at[d - 1], fin_b.at[d - 1], b2_s.at[d - 1], b2_r.at[d - 1], at_x(d))
            )
        if i < spans - 1:
            d = far_first(spans)[i]
            sum_a[d - 1] = sum_top(d).astype(BF16)
            a2_copies.append(
                send(sum_a.at[d - 1], fin_a.at[d - 1], a2_s.at[d - 1], a2_r.at[d - 1], at_y(d))
            )
    share_b, share_a = sum_low(0), sum_top(0)
    for copy in a2_copies + b2_copies:
        copy.wait_recv()
    for d in range(spans - 1):
        share_a = share_a + fin_a[d].astype(F32)
    for d in range(sects - 1):
        share_b = share_b + fin_b[d].astype(F32)
    share = jnp.concatenate([share_a, share_b], 0).astype(BF16)

    grad_attn = jnp.zeros((cols, patches), F32)
    for p in range(4):
        grad_attn = grad_attn + dot(share[:, p * cols : (p + 1) * cols], spread[p], FIRST)
    row_delta = jnp.sum(grad_attn * attended, 0, keepdims=True)
    grad_attn = grad_attn.astype(BF16)
    back_copies = []
    q = qs[...]

    def give_back(block, kind, term):
        side = block // 2
        back[side, kind] = term.astype(BF16)
        back_copies.append(
            send(
                back.at[side, kind],
                back_in.at[1 - side, kind],
                back_s.at[side, kind],
                back_r.at[1 - side, kind],
                at_g(block - 1),
            )
        )

    def value_term(block):
        return dot(grad_attn, probs_low[block], LAST)

    def score_term(block):
        grad_probs = dot(vx[block], grad_attn, FIRST)
        return (probs[block] * (grad_probs - row_delta)).astype(BF16)

    for block in (0, 2):
        give_back(block, 1, value_term(block))
    grad_query = jnp.zeros((cols, patches), F32)
    for block in (0, 2):
        score_part = score_term(block)
        give_back(block, 0, dot(q, score_part, LAST) * scale)
        grad_query = grad_query + dot(kx[block], score_part)
    score_part = score_term(1)
    key_part = dot(q, score_part, LAST) * scale
    value_part = value_term(1)
    grad_query = grad_query + dot(kx[1], score_part)
    out_q[...] = (grad_query * scale).astype(BF16)
    for copy in back_copies:
        copy.wait_recv()
    for side in range(2):
        key_part = key_part + back_in[side, 0].astype(F32)
        value_part = value_part + back_in[side, 1].astype(F32)
    out_k[...] = key_part.astype(BF16)
    out_v[...] = value_part.astype(BF16)
    for copy in sent:
        copy.wait_send()


def move(*refs):
    half = len(refs) // 2
    for source, target in zip(refs[:half], refs[half:]):
        target[...] = source[...]


def on_device(
    grad_out, destination, w_down, pre_act, w_up, queries, key_states, value_states, lengths
):
    sects, groups, spans = (lax.axis_size(a) for a in ("sect", "grp", "span"))
    rows, merged = grad_out.shape
    merge_rows, hidden = w_up.shape
    cols = queries.shape[1]
    patches = 4 * rows
    near = 8 if groups % 8 == 0 and groups > 8 else 2
    far = groups // near
    cap = rows // min(groups, rows // 2)
    slots = groups * cap
    split = (rows * 5 // 8 // 16) * 16 if rows >= 32 else rows // 2
    width = 4 * cols
    wide = hidden + LABEL_LANES
    dma = pltpu.SemaphoreType.DMA
    vmem = pltpu.VMEM
    some = pl.BlockSpec(memory_space=pl.ANY)
    out = jax.ShapeDtypeStruct((cols, patches), BF16)
    sizes = (sects, groups, spans, near, far, cap, split)
    outs = pl.pallas_call(
        functools.partial(kernel, sizes),
        out_shape=(out, out, out),
        in_specs=[some] * 9,
        out_specs=[pl.BlockSpec(memory_space=pltpu.VMEM)] * 3,
        scratch_shapes=[
            vmem((rows, merged), BF16),
            vmem(w_down.shape, BF16),
            vmem((hidden, merge_rows), BF16),
            vmem((sects * spans, hidden, width), BF16),
            vmem((rows, hidden), BF16),
            vmem((cols, patches), BF16),
            vmem((3, cols, patches), BF16),
            vmem((3, cols, patches), BF16),
            vmem((1, rows), jnp.int32),
            vmem((1, lengths.shape[0]), jnp.int32),
            vmem((spans - 1, rows, hidden), BF16),
            vmem((spans - 1, rows, hidden), BF16),
            vmem((slots, wide), BF16),
            vmem((slots, wide), BF16),
            vmem((slots, wide), BF16),
            vmem((slots, wide), BF16),
            vmem((sects, spans, rows, width), BF16),
            vmem((sects - 1, spans, split, width), BF16),
            vmem((spans - 1, sects, rows - split, width), BF16),
            vmem((spans - 1, split, width), BF16),
            vmem((sects - 1, rows - split, width), BF16),
            vmem((spans - 1, split, width), BF16),
            vmem((sects - 1, rows - split, width), BF16),
            vmem((2, 2, cols, patches), BF16),
            vmem((2, 2, cols, patches), BF16),
            vmem((3, patches, patches), F32),
            vmem((3, patches, patches), BF16),
            vmem((slots, rows), BF16),
            vmem((slots, slots), BF16),
            vmem((4, rows, patches), BF16),
            vmem((rows, hidden), F32),
            vmem((rows, hidden), F32),
            pltpu.SemaphoreType.REGULAR((2, 4)),
            dma((8,)),
            dma((spans,)),
            dma((spans - 1,)),
            dma((spans - 1,)),
            dma((4,)),
            dma((4,)),
            dma((near - 1,)),
            dma((near - 1,)),
            dma((far - 1,)),
            dma((far - 1,)),
            dma((sects - 1, spans)),
            dma((sects - 1, spans)),
            dma((spans - 1, sects)),
            dma((spans - 1, sects)),
            dma((spans - 1,)),
            dma((spans - 1,)),
            dma((sects - 1,)),
            dma((sects - 1,)),
            dma((2, 2)),
            dma((2, 2)),
        ],
        compiler_params=pltpu.CompilerParams(
            collective_id=0, has_side_effects=True, vmem_limit_bytes=60 * 1024 * 1024
        ),
        name="merger_attention_backward",
    )(
        grad_out,
        destination.reshape(1, rows),
        w_down,
        pre_act,
        w_up.T,
        queries.T,
        key_states.T,
        value_states.T,
        lengths.reshape(1, lengths.shape[0]),
    )
    outs = pl.pallas_call(
        move,
        out_shape=(out, out, out),
        in_specs=[pl.BlockSpec(memory_space=pltpu.VMEM)] * 3,
        out_specs=[pl.BlockSpec(memory_space=pltpu.VMEM)] * 3,
        name="gradients_out",
    )(*outs)
    return tuple(each.T for each in outs)


def solution(mesh):
    placed = (
        P("grp", "span"),
        P("grp"),
        P("sect", "span"),
        P("grp", ("sect", "span")),
        P(None, ("sect", "span")),
        P("grp", ("sect", "span")),
        P("grp", ("sect", "span")),
        P("grp", ("sect", "span")),
        P(),
    )
    return jax.shard_map(
        on_device,
        mesh=mesh,
        in_specs=placed,
        out_specs=(
            P("grp", ("sect", "span")),
            P("grp", ("sect", "span")),
            P("grp", ("sect", "span")),
        ),
        check_vma=False,
    )
```

```python
import functools

import jax
import jax.numpy as jnp
from jax import lax
from jax.experimental import pallas as pl
from jax.experimental.pallas import tpu as pltpu
from jax.sharding import PartitionSpec as P

HEAD_DIM = 80
LABEL_LANES = 64
BF16 = jnp.bfloat16
F32 = jnp.float32
LAST = (((1,), (1,)), ((), ()))
FIRST = (((0,), (0,)), ((), ()))


def dot(a, b, dims=(((1,), (0,)), ((), ()))):
    return lax.dot_general(a, b, dims, preferred_element_type=F32)


def iota(shape, dim):
    return lax.broadcasted_iota(jnp.int32, shape, dim)


def gelu_slope(values):
    normal_cdf = 0.5 * (1.0 + lax.erf(values * 0.7071067811865476))
    return normal_cdf + values * jnp.exp(-0.5 * values * values) * 0.3989422804014327


def log2(n):
    return n.bit_length() - 1


def far_first(n):
    return sorted(range(1, n), key=lambda d: -min(d, n - d))


def token_packing(dest, rows, near, far, cap):
    where_to = dest.astype(F32)
    group = jnp.floor((where_to + 0.5) * (1.0 / rows))
    place = where_to - group * rows
    square = (rows, rows)
    across = jnp.broadcast_to(group, square)
    down = jnp.sum(jnp.where(iota(square, 0) == iota(square, 1), across, 0.0), 1, keepdims=True)
    earlier = (down == across) & (iota(square, 0) < iota(square, 1))
    copy = jnp.sum(jnp.where(earlier, 1.0, 0.0), 0, keepdims=True)
    group_hi = jnp.floor((group + 0.5) * (1.0 / near))
    slot = (group - group_hi * near) * (far * cap) + group_hi * cap + copy
    slots = near * far * cap
    hit = iota((slots, rows), 0).astype(F32) == slot
    label = jnp.sum(jnp.where(hit, place + 1.0, 0.0), 1, keepdims=True)
    return jnp.where(hit, 1.0, 0.0).astype(BF16), label


def image_ids(lengths, group, rows, tokens):
    images = lengths.shape[1]
    square = (images, images)
    sizes = jnp.broadcast_to(lengths.astype(F32), square)
    row, col = iota(square, 0), iota(square, 1)
    sizes_down = jnp.sum(jnp.where(row == col, sizes, 0.0), 1, keepdims=True)
    ends_down = jnp.sum(jnp.where(col <= row, sizes, 0.0), 1, keepdims=True)
    ends_across = jnp.sum(jnp.where(row <= col, sizes_down, 0.0), 0, keepdims=True)
    base = group * rows
    own = (base + (iota((1, 4 * rows), 1) >> 2)).astype(F32)
    near = (base - rows + (iota((12 * rows, 1), 0) >> 2)).astype(F32)
    own_image = jnp.sum(jnp.where(ends_down <= own, 1.0, 0.0), 0, keepdims=True)
    near_image = jnp.sum(jnp.where(ends_across <= near, 1.0, 0.0), 1, keepdims=True)
    inside = (near >= 0.0) & (near < float(tokens))
    return own_image, jnp.where(inside, near_image, -1.0)


def kernel(
    sizes,
    grad_out,
    dest,
    w_down,
    pre_act,
    w_up,
    queries,
    keys,
    values,
    lengths,
    out_q,
    out_k,
    out_v,
    go,
    wd,
    wt,
    wu,
    pre,
    qs,
    kx,
    vx,
    dst,
    lens,
    part,
    part_in,
    near_out,
    near_in,
    far_out,
    far_in,
    mix,
    mix_a,
    mix_b,
    fin_a,
    fin_b,
    sum_a,
    sum_b,
    back,
    back_in,
    probs,
    probs_low,
    pack,
    swap,
    spread,
    slopes,
    own_part,
    ready,
    load_sem,
    down_sem,
    part_s,
    part_r,
    halo_s,
    halo_r,
    near_s,
    near_r,
    far_s,
    far_r,
    a1_s,
    a1_r,
    b1_s,
    b1_r,
    a2_s,
    a2_r,
    b2_s,
    b2_r,
    back_s,
    back_r,
):
    sects, groups, spans, near, far, cap, split = sizes
    rows = grad_out.shape[0]
    hidden = w_up.shape[0]
    cols = queries.shape[0]
    patches = 4 * rows
    x, g, y = lax.axis_index("sect"), lax.axis_index("grp"), lax.axis_index("span")
    g_hi, g_lo = g // near, g % near

    def at_x(d):
        return ((x + d) % sects, g, y)

    def at_y(d):
        return (x, g, (y + d) % spans)

    def at_near(d):
        return (x, g_hi * near + (g_lo + d) % near, y)

    def at_far(d):
        return (x, ((g_hi + d) % far) * near + g_lo, y)

    def at_g(d):
        return (x, (g + d + groups) % groups, y)

    sent = []

    def send(src, to, send_sem, recv_sem, peer):
        copy = pltpu.make_async_remote_copy(
            src_ref=src,
            dst_ref=to,
            send_sem=send_sem,
            recv_sem=recv_sem,
            device_id=peer,
            device_id_type=pl.DeviceIdType.MESH,
        )
        copy.start()
        sent.append(copy)
        return copy

    def load(src, to, sem):
        copy = pltpu.make_async_copy(src, to, sem)
        copy.start()
        return copy

    order_y = far_first(spans) + [0]
    load_go = load(grad_out, go, load_sem.at[0])
    load_dst = load(dest, dst, load_sem.at[1])
    load_wd = []

    def load_chunk(d):
        chunk = pl.ds(pl.multiple_of(((y + d) % spans) * hidden, 16), hidden)
        load_wd.append(load(w_down.at[chunk, :], wd.at[chunk, :], down_sem.at[d]))

    for d in order_y[:2]:
        load_chunk(d)

    barrier = pltpu.get_barrier_semaphore()
    far_steps = sorted({1 % far, far - 1})
    peers = [at_far(d) for d in far_steps]
    peers += [at_y(d) for d in range(1, spans)]
    peers += [at_near(d) for d in range(1, near)]
    peers += [at_g(1), at_g(-1)]
    peers += [at_x(d) for d in range(1, sects)]
    def signal(sem, peer):
        pl.semaphore_signal(sem, inc=1, device_id=peer, device_id_type=pl.DeviceIdType.MESH)

    for peer in peers:
        signal(barrier, peer)

    load_go.wait()
    part_copies = []
    for i, d in enumerate(order_y):
        load_wd[i].wait()
        if i + 2 < len(order_y):
            load_chunk(order_y[i + 2])
        elif i + 2 == len(order_y):
            load_k = load(keys, kx.at[1], load_sem.at[4])
            load_v = load(values, vx.at[1], load_sem.at[5])
            load_len = load(lengths, lens, load_sem.at[2])
            load_q = load(queries, qs, load_sem.at[3])
            load_pre = load(pre_act, pre, load_sem.at[6])
        chunk = pl.ds(pl.multiple_of(((y + d) % spans) * hidden, 16), hidden)
        product = dot(go[...], wd[chunk, :], LAST)
        if d == 0:
            own_part[...] = product
            continue
        part[d - 1] = product.astype(BF16)
        if not part_copies:
            pl.semaphore_wait(barrier, len(peers))
            for j, step in enumerate(far_steps):
                signal(ready.at[0, j], at_far(step))
        part_copies.append(
            send(part.at[d - 1], part_in.at[d - 1], part_s.at[d - 1], part_r.at[d - 1], at_y(d))
        )
    load_wt = load(w_up, wt, load_sem.at[7])
    load_k.wait()
    load_v.wait()
    halo_copies = []
    for i, (full, step) in enumerate(((kx, 1), (vx, 1), (kx, -1), (vx, -1))):
        land = full.at[0 if step == 1 else 2]
        halo_copies.append(send(full.at[1], land, halo_s.at[i], halo_r.at[i], at_g(step)))
    load_dst.wait()
    pack[...], label = token_packing(dst[...], rows, near, far, cap)
    near_out[:, hidden:] = jnp.broadcast_to(label, (near * far * cap, LABEL_LANES)).astype(BF16)
    slots = near * far * cap
    near_rows, far_rows = far * cap, near * cap
    out_row = iota((slots, slots), 0)
    in_row = iota((slots, slots), 1)
    source = ((out_row >> log2(cap)) & (near - 1)) * near_rows
    source = source + (out_row >> log2(far_rows)) * cap + (out_row & (cap - 1))
    swap[...] = jnp.where(source == in_row, 1.0, 0.0).astype(BF16)
    for i in range(len(far_steps)):
        pl.semaphore_wait(ready.at[0, i], 1)
    second = [d for d in (1, far - 1, 2, far - 2) if far > 2 and d < far]
    second = sorted(set(second))
    for i, d in enumerate(second):
        signal(ready.at[1, i], at_far(d))

    total = own_part[...]
    for d, copy in zip(far_first(spans), part_copies):
        copy.wait_recv()
        total = total + part_in[d - 1].astype(F32)
    near_out[:, :hidden] = dot(pack[...], total.astype(BF16)).astype(BF16)
    near_copies = []
    for d in range(near - 1, 0, -1):
        block = pl.ds(pl.multiple_of(((g_lo + d) % near) * near_rows, near_rows), near_rows)
        near_copies.append(
            send(
                near_out.at[block, :],
                near_in.at[pl.ds(d * near_rows, near_rows), :],
                near_s.at[d - 1],
                near_r.at[d - 1],
                at_near(d),
            )
        )
    mine = pl.ds(pl.multiple_of(g_lo * near_rows, near_rows), near_rows)
    near_in[pl.ds(0, near_rows), :] = near_out[mine, :]
    for copy in near_copies:
        copy.wait_recv()
    far_out[...] = dot(swap[...], near_in[...]).astype(BF16)
    for i in range(len(second)):
        pl.semaphore_wait(ready.at[1, i], 1)
    far_copies = []

    def release(d):
        block = pl.ds(pl.multiple_of(((g_hi + d) % far) * far_rows, far_rows), far_rows)
        far_copies.append(
            send(
                far_out.at[block, :],
                far_in.at[pl.ds(d * far_rows, far_rows), :],
                far_s.at[d - 1],
                far_r.at[d - 1],
                at_far(d),
            )
        )
    waves = [[d for d in far_first(far) if min(d, far - d) == k] for k in range(far // 2, 0, -1)]
    waves += [[]] * (4 - len(waves))
    for d in waves[0] + waves[1]:
        release(d)
    mine = pl.ds(pl.multiple_of(g_hi * far_rows, far_rows), far_rows)
    far_in[pl.ds(0, far_rows), :] = far_out[mine, :]

    scale = HEAD_DIM ** (-0.5)
    width = 4 * cols
    load_q.wait()
    for copy in halo_copies:
        copy.wait_recv()
    load_len.wait()
    own_image, near_image = image_ids(lens[...], g, rows, rows * groups)
    top_score = None
    for block in range(3):
        scores = dot(kx[block], qs[...], FIRST) * scale
        image = near_image[block * patches : (block + 1) * patches]
        scores = jnp.where(image == own_image, scores, -jnp.inf)
        probs[block] = scores
        top = jnp.max(scores, 0, keepdims=True)
        top_score = top if top_score is None else jnp.maximum(top_score, top)
    weight_sum = jnp.zeros((1, patches), F32)
    for block in range(3):
        weights = jnp.exp(probs[block] - top_score)
        probs[block] = weights
        weight_sum = weight_sum + jnp.sum(weights, 0, keepdims=True)
    attended = jnp.zeros((cols, patches), F32)
    for block in range(3):
        weights = probs[block] / weight_sum
        probs[block] = weights
        probs_low[block] = weights.astype(BF16)
        attended = attended + dot(vx[block], probs_low[block])
    load_pre.wait()
    slopes[...] = gelu_slope(pre[...].astype(F32))
    token, patch = iota((rows, patches), 0), iota((rows, patches), 1)
    for p in range(4):
        spread[p] = jnp.where(patch == 4 * token + p, 1.0, 0.0).astype(BF16)
    load_wt.wait()
    step_rows = 32

    def regroup(i, carry):
        some = pl.ds(pl.multiple_of(i * step_rows, step_rows), step_rows)
        for d in range(sects * spans):
            for p in range(4):
                start = (p * sects * spans + d) * cols
                wu[d, some, p * cols : (p + 1) * cols] = wt[some, start : start + cols]
        return carry

    halves = hidden // step_rows // 2
    lax.fori_loop(0, halves, regroup, 0)
    for d in waves[2]:
        release(d)
    lax.fori_loop(halves, hidden // step_rows, regroup, 0)

    for d in waves[3]:
        release(d)

    for copy in far_copies:
        copy.wait_recv()
    arrived = far_in[...]
    place = arrived[:, hidden : hidden + 1].astype(F32)
    unpacker = jnp.where(place == (iota((slots, rows), 1) + 1).astype(F32), 1.0, 0.0)
    grad_hidden = dot(unpacker.astype(BF16), arrived[:, :hidden], FIRST)
    grad_pre = (grad_hidden * slopes[...]).astype(BF16)
    top, low = pl.ds(0, split), pl.ds(split, rows - split)
    a_copies, b_copies = {}, {}
    pairs = [(dx, dy) for dx in far_first(sects) for dy in far_first(spans)]
    pairs.sort(key=lambda d: -min(d[0], sects - d[0]) - min(d[1], spans - d[1]))
    pairs += [(dx, 0) for dx in far_first(sects)] + [(0, dy) for dy in far_first(spans)]
    for dx, dy in pairs + [(0, 0)]:
        owner = ((x + dx) % sects) * spans + (y + dy) % spans
        mix[dx, dy] = dot(grad_pre, wu[owner]).astype(BF16)
        if dx:
            a_copies[dx, dy] = send(
                mix.at[dx, dy, top, :],
                mix_a.at[dx - 1, dy],
                a1_s.at[dx - 1, dy],
                a1_r.at[dx - 1, dy],
                at_x(dx),
            )
        if dy:
            b_copies[dx, dy] = send(
                mix.at[dx, dy, low, :],
                mix_b.at[dy - 1, dx],
                b1_s.at[dy - 1, dx],
                b1_r.at[dy - 1, dx],
                at_y(dy),
            )
    a2_copies, b2_copies = [], []

    def sum_top(dy):
        total = mix[0, dy, top, :].astype(F32)
        for dx in far_first(sects):
            a_copies[dx, dy].wait_recv()
            total = total + mix_a[dx - 1, dy].astype(F32)
        return total

    def sum_low(dx):
        total = mix[dx, 0, low, :].astype(F32)
        for dy in far_first(spans):
            b_copies[dx, dy].wait_recv()
            total = total + mix_b[dy - 1, dx].astype(F32)
        return total

    for i in range(max(sects, spans) - 1):
        if i < sects - 1:
            d = far_first(sects)[i]
            sum_b[d - 1] = sum_low(d).astype(BF16)
            b2_copies.append(
                send(sum_b.at[d - 1], fin_b.at[d - 1], b2_s.at[d - 1], b2_r.at[d - 1], at_x(d))
            )
        if i < spans - 1:
            d = far_first(spans)[i]
            sum_a[d - 1] = sum_top(d).astype(BF16)
            a2_copies.append(
                send(sum_a.at[d - 1], fin_a.at[d - 1], a2_s.at[d - 1], a2_r.at[d - 1], at_y(d))
            )
    share_b, share_a = sum_low(0), sum_top(0)
    for copy in a2_copies + b2_copies:
        copy.wait_recv()
    for d in range(spans - 1):
        share_a = share_a + fin_a[d].astype(F32)
    for d in range(sects - 1):
        share_b = share_b + fin_b[d].astype(F32)
    share = jnp.concatenate([share_a, share_b], 0).astype(BF16)

    grad_attn = jnp.zeros((cols, patches), F32)
    for p in range(4):
        grad_attn = grad_attn + dot(share[:, p * cols : (p + 1) * cols], spread[p], FIRST)
    row_delta = jnp.sum(grad_attn * attended, 0, keepdims=True)
    grad_attn = grad_attn.astype(BF16)
    back_copies = []
    q = qs[...]

    def give_back(block, kind, term):
        side = block // 2
        back[side, kind] = term.astype(BF16)
        back_copies.append(
            send(
                back.at[side, kind],
                back_in.at[1 - side, kind],
                back_s.at[side, kind],
                back_r.at[1 - side, kind],
                at_g(block - 1),
            )
        )

    def value_term(block):
        return dot(grad_attn, probs_low[block], LAST)

    def score_term(block):
        grad_probs = dot(vx[block], grad_attn, FIRST)
        return (probs[block] * (grad_probs - row_delta)).astype(BF16)

    for block in (0, 2):
        give_back(block, 1, value_term(block))
    grad_query = jnp.zeros((cols, patches), F32)
    for block in (0, 2):
        score_part = score_term(block)
        give_back(block, 0, dot(q, score_part, LAST) * scale)
        grad_query = grad_query + dot(kx[block], score_part)
    score_part = score_term(1)
    key_part = dot(q, score_part, LAST) * scale
    value_part = value_term(1)
    grad_query = grad_query + dot(kx[1], score_part)
    out_q[...] = (grad_query * scale).astype(BF16)
    for copy in back_copies:
        copy.wait_recv()
    for side in range(2):
        key_part = key_part + back_in[side, 0].astype(F32)
        value_part = value_part + back_in[side, 1].astype(F32)
    out_k[...] = key_part.astype(BF16)
    out_v[...] = value_part.astype(BF16)
    for copy in sent:
        copy.wait_send()


def move(*refs):
    half = len(refs) // 2
    for source, target in zip(refs[:half], refs[half:]):
        target[...] = source[...]


def on_device(
    grad_out, destination, w_down, pre_act, w_up, queries, key_states, value_states, lengths
):
    sects, groups, spans = (lax.axis_size(a) for a in ("sect", "grp", "span"))
    rows, merged = grad_out.shape
    merge_rows, hidden = w_up.shape
    cols = queries.shape[1]
    patches = 4 * rows
    near = 8 if groups % 8 == 0 and groups > 8 else 2
    far = groups // near
    cap = rows // min(groups, rows // 2)
    slots = groups * cap
    split = (rows * 5 // 8 // 16) * 16 if rows >= 32 else rows // 2
    width = 4 * cols
    wide = hidden + LABEL_LANES
    dma = pltpu.SemaphoreType.DMA
    vmem = pltpu.VMEM
    some = pl.BlockSpec(memory_space=pl.ANY)
    out = jax.ShapeDtypeStruct((cols, patches), BF16)
    sizes = (sects, groups, spans, near, far, cap, split)
    outs = pl.pallas_call(
        functools.partial(kernel, sizes),
        out_shape=(out, out, out),
        in_specs=[some] * 9,
        out_specs=[pl.BlockSpec(memory_space=pltpu.VMEM)] * 3,
        scratch_shapes=[
            vmem((rows, merged), BF16),
            vmem(w_down.shape, BF16),
            vmem((hidden, merge_rows), BF16),
            vmem((sects * spans, hidden, width), BF16),
            vmem((rows, hidden), BF16),
            vmem((cols, patches), BF16),
            vmem((3, cols, patches), BF16),
            vmem((3, cols, patches), BF16),
            vmem((1, rows), jnp.int32),
            vmem((1, lengths.shape[0]), jnp.int32),
            vmem((spans - 1, rows, hidden), BF16),
            vmem((spans - 1, rows, hidden), BF16),
            vmem((slots, wide), BF16),
            vmem((slots, wide), BF16),
            vmem((slots, wide), BF16),
            vmem((slots, wide), BF16),
            vmem((sects, spans, rows, width), BF16),
            vmem((sects - 1, spans, split, width), BF16),
            vmem((spans - 1, sects, rows - split, width), BF16),
            vmem((spans - 1, split, width), BF16),
            vmem((sects - 1, rows - split, width), BF16),
            vmem((spans - 1, split, width), BF16),
            vmem((sects - 1, rows - split, width), BF16),
            vmem((2, 2, cols, patches), BF16),
            vmem((2, 2, cols, patches), BF16),
            vmem((3, patches, patches), F32),
            vmem((3, patches, patches), BF16),
            vmem((slots, rows), BF16),
            vmem((slots, slots), BF16),
            vmem((4, rows, patches), BF16),
            vmem((rows, hidden), F32),
            vmem((rows, hidden), F32),
            pltpu.SemaphoreType.REGULAR((2, 4)),
            dma((8,)),
            dma((spans,)),
            dma((spans - 1,)),
            dma((spans - 1,)),
            dma((4,)),
            dma((4,)),
            dma((near - 1,)),
            dma((near - 1,)),
            dma((far - 1,)),
            dma((far - 1,)),
            dma((sects - 1, spans)),
            dma((sects - 1, spans)),
            dma((spans - 1, sects)),
            dma((spans - 1, sects)),
            dma((spans - 1,)),
            dma((spans - 1,)),
            dma((sects - 1,)),
            dma((sects - 1,)),
            dma((2, 2)),
            dma((2, 2)),
        ],
        compiler_params=pltpu.CompilerParams(
            collective_id=0, has_side_effects=True, vmem_limit_bytes=60 * 1024 * 1024
        ),
        name="merger_attention_backward",
    )(
        grad_out,
        destination.reshape(1, rows),
        w_down,
        pre_act,
        w_up.T,
        queries.T,
        key_states.T,
        value_states.T,
        lengths.reshape(1, lengths.shape[0]),
    )
    outs = pl.pallas_call(
        move,
        out_shape=(out, out, out),
        in_specs=[pl.BlockSpec(memory_space=pltpu.VMEM)] * 3,
        out_specs=[pl.BlockSpec(memory_space=pltpu.VMEM)] * 3,
        name="gradients_out",
    )(*outs)
    return tuple(each.T for each in outs)


def solution(mesh):
    placed = (
        P("grp", "span"),
        P("grp"),
        P("sect", "span"),
        P("grp", ("sect", "span")),
        P(None, ("sect", "span")),
        P("grp", ("sect", "span")),
        P("grp", ("sect", "span")),
        P("grp", ("sect", "span")),
        P(),
    )
    return jax.shard_map(
        on_device,
        mesh=mesh,
        in_specs=placed,
        out_specs=(
            P("grp", ("sect", "span")),
            P("grp", ("sect", "span")),
            P("grp", ("sect", "span")),
        ),
        check_vma=False,
    )
```
